32 devices in a mesh: dp: 8 (over z, y), tensor: 4 (over x, core).
Axes of the slice: x: 2, y: 2, z: 4, core: 2. Of those that a mesh axis runs over, the one named last changes fastest.
Arguments:
- tokens: bfloat16 [3, 4096, 1536], P(None, ('dp', 'tensor')), may hold values from -6 to 6
- lengths: int32 [3, 32, 6], P(None, ('dp', 'tensor')), may hold values from 1 to 64, 128 in all within a row
- first_gain: bfloat16 [1536], P(('dp', 'tensor')), may hold values from 0.099609375 to 1.8984375
- query_weight: bfloat16 [1536, 1536], P(('dp', 'tensor')), may hold values from -0.15625 to 0.15625
- key_weight: bfloat16 [1536, 768], P(('dp', 'tensor')), may hold values from -0.15625 to 0.15625
- value_weight: bfloat16 [1536, 768], P(('dp', 'tensor')), may hold values from -0.15625 to 0.15625
- output_weight: bfloat16 [1536, 1536], P(('dp', 'tensor')), may hold values from -0.4375 to 0.4375
- second_gain: bfloat16 [1536], P(('dp', 'tensor')), may hold values from 0.099609375 to 1.8984375
- gate_weight: bfloat16 [1536, 4096], P('dp', 'tensor'), may hold values from -0.15625 to 0.15625
- up_weight: bfloat16 [1536, 4096], P('dp', 'tensor'), may hold values from -0.15625 to 0.15625
- down_weight: bfloat16 [4096, 1536], P('tensor', 'dp'), may hold values from -0.09375 to 0.09375
- cotangent: bfloat16 [3, 4096, 1536], P(None, ('dp', 'tensor')), may hold values from -6 to 6
Outputs:
- layer_out: bfloat16 [3, 4096, 1536], P(None, ('dp', 'tensor'))
- input_grad: float32 [3, 4096, 1536], P(None, ('dp', 'tensor'))
- first_gain_grad: float32 [1536], P(('dp', 'tensor'))
- query_grad: float32 [1536, 1536], P(('dp', 'tensor'))
- key_grad: float32 [1536, 768], P(('dp', 'tensor'))
- value_grad: float32 [1536, 768], P(('dp', 'tensor'))
- output_grad: float32 [1536, 1536], P(('dp', 'tensor'))
- second_gain_grad: float32 [1536], P(('dp', 'tensor'))
- gate_grad: float32 [1536, 4096], P('dp', 'tensor')
- up_grad: float32 [1536, 4096], P('dp', 'tensor')
- down_grad: float32 [4096, 1536], P('tensor', 'dp')
The draws below stay inside these ranges and needn't reach their ends.
Inputs may be any that keep to these rules, and one draw needn't show every extreme that they name: Row lengths[m, p] splits the 128 rows of pack p of micro-batch m into 6 runs in order, summing to 128; the first 5 runs are sequences, the last is padding; no run is longer than 64 rows.
All inputs are finite; a program needn't handle non-finite values.
Results may differ from the reference program's by a relative error of at most 0.013.
Values may be sent and summed in bfloat16 or wider, within the bound.
No kernel may reach another device: no remote copies, remote signals or barrier semaphores. Data moves between devices by JAX's collectives and lax.ppermute only.
A program may use at most 192 MiB of HBM per device.

```python
import math
import jax
import jax.numpy as jnp
import numpy as np
from jax import lax

D = 1536
HEADS = 16
KV_HEADS = 8
HEAD = 96
FF = 4096
TOK_MB = 128
MB = 3
SLOTS = 6
QW = 1536
KW = 768
PACKS = 32
ROWS = 4096


def spiked(array, key, source, target, parts, factor):
    owner, partner = [(jnp.arange(array.shape[dim]) // (array.shape[dim] // parts)).reshape([-1 if axis == dim else 1 for axis in range(array.ndim)]) for dim in (source, target)]
    chosen = jax.random.permutation(key, parts)[partner]
    strong = (owner == chosen) | (owner == (partner + parts // 2) % parts)
    return jnp.where(strong, factor * array, array)


def shard_levels(own_key, shape, shards, least, high):
    loudness, own = 1.0, jax.random.fold_in(own_key, 6)
    for axis_at, parts in shards:
        steps = jnp.exp(jax.random.uniform(jax.random.fold_in(own, axis_at), (parts,), jnp.float32, least / len(shards), high / len(shards)))
        loudness = loudness * jnp.repeat(steps, shape[axis_at] // parts).reshape([-1 if axis == axis_at else 1 for axis in range(len(shape))])
    return loudness


def profile(number_of, total, most, slope):
    weights = [(1 << 20) // math.isqrt(rank ** slope) + 1 for rank in range(2, number_of + 1)]
    spare, given = total - most - (number_of - 1), [1] * (number_of - 1)
    while spare > 0:
        candidates = [i for i in range(number_of - 1) if given[i] < most]
        mass, budget = sum([weights[i] for i in candidates]), spare
        for i in candidates:
            extra = min(most - given[i], max(1, budget * weights[i] // mass), spare)
            given[i] = given[i] + extra
            spare = spare - extra
    return np.array([most] + given)


def uneven_parts(stream_key, number_of, total, bound, lean):
    if number_of == 2:
        one = jax.random.randint(stream_key, (), max(1, total - bound), min(bound, total - 1) + 1)
        return jnp.stack([one, total - one])
    sizes = jnp.asarray(profile(number_of, total, bound, lean), jnp.int32)
    twos = (number_of - 1) // 2
    giver, taker = sizes[1:1 + 2 * twos:2], sizes[2:2 + 2 * twos:2]
    room = jnp.minimum(giver - 1, bound - taker)
    shifted = jax.random.randint(jax.random.fold_in(stream_key, 1), (twos,), 0, 1 << 20) % (room + 1)
    sizes = sizes.at[1:1 + 2 * twos:2].set(giver - shifted).at[2:2 + 2 * twos:2].set(taker + shifted)
    return sizes[jax.random.permutation(jax.random.fold_in(stream_key, 2), number_of)]


def normal_values(own_key, shape, width, limit, split=(), kind=jnp.bfloat16):
    drawn = width * jax.random.normal(own_key, shape, jnp.float32)
    if split:
        drawn = drawn * shard_levels(own_key, shape, split, -0.22, 0.18)
    return jnp.clip(drawn, -limit, limit).astype(kind)


def noise_with(stream_key, dims, deviation, limit, cuts, heavy, held_as=jnp.bfloat16):
    values = deviation * jax.random.normal(stream_key, dims, jnp.float32)
    if cuts:
        values = values * shard_levels(stream_key, dims, cuts, -0.22, 0.18)
    return jnp.clip(spiked(values, jax.random.fold_in(stream_key, 3), *heavy), -limit, limit).astype(held_as)


def setup_inputs(seed: int = 0) -> dict:
    splits = jax.random.split(jax.random.key(seed), 13)
    return {
        "tokens": noise_with(splits[0], (MB, ROWS, D), 1.0, 6.0, ((1, 32),), (1, 2, 32, 2.75)),
        "lengths": jax.vmap(lambda own: uneven_parts(own, SLOTS, TOK_MB, TOK_MB // 2, 2))(jax.random.split(splits[1], MB * PACKS)).reshape((MB, PACKS, SLOTS)).astype(jnp.int32),
        "first_gain": jnp.clip(1.0 + 0.18 * jax.random.normal(splits[2], (D,), jnp.float32), 0.099609375, 1.8984375).astype(jnp.bfloat16),
        "query_weight": normal_values(splits[3], (D, QW), D ** -0.5, 0.15625, ((0, 32),)),
        "key_weight": normal_values(splits[4], (D, KW), D ** -0.5, 0.15625, ((0, 32),)),
        "value_weight": normal_values(splits[5], (D, KW), D ** -0.5, 0.15625, ((0, 32),)),
        "output_weight": normal_values(splits[6], (QW, D), (QW // 8) ** -0.5, 0.4375, ((0, 32),)),
        "second_gain": jnp.clip(1.0 + 0.18 * jax.random.normal(splits[7], (D,), jnp.float32), 0.099609375, 1.8984375).astype(jnp.bfloat16),
        "gate_weight": normal_values(splits[8], (D, FF), D ** -0.5, 0.15625, ((0, 8), (1, 4))),
        "up_weight": normal_values(splits[9], (D, FF), D ** -0.5, 0.15625, ((0, 8), (1, 4))),
        "down_weight": normal_values(splits[10], (FF, D), FF ** -0.5, 0.09375, ((0, 4), (1, 8))),
        "cotangent": noise_with(splits[11], (MB, ROWS, D), 1.0, 6.0, ((1, 32),), (1, 2, 32, 2.75)),
    }


EPSILON = 1e-05
ROPE_BASE = 100000.0
HIGHEST = lax.Precision.HIGHEST

@jax.custom_vjp
def low(v):
    return lax.optimization_barrier(v.astype(jnp.bfloat16)).astype(jnp.float32)

@jax.custom_vjp
def low_back(v):
    return v

def low_keep(v):
    return (low(v), None)

def low_pass(kept, grad):
    return (grad,)

def back_keep(v):
    return (v, None)

def back_low(kept, grad):
    return (low(grad),)
low.defvjp(low_keep, low_pass)
low_back.defvjp(back_keep, back_low)

def matmul(left_side, right_side):
    return jnp.dot(left_side, right_side, precision=HIGHEST, preferred_element_type=jnp.float32)

def pack_layout(seq_lengths, row_count):
    seq_ends = jnp.cumsum(seq_lengths).astype(jnp.int32)
    seq_starts = (seq_ends - seq_lengths).astype(jnp.int32)
    row_index = jnp.arange(row_count, dtype=jnp.int32)
    segment = lax.optimization_barrier(jnp.sum((row_index[:, None] >= seq_ends[None, :]).astype(jnp.int32), axis=1)).astype(jnp.int32)
    owner_hot = segment[:, None] == jnp.arange(seq_lengths.shape[0], dtype=jnp.int32)[None, :]
    position = (row_index - lax.optimization_barrier(jnp.sum(jnp.where(owner_hot, seq_starts[None, :], 0), axis=1))).astype(jnp.int32)
    return (segment, position)

def rotary_tables(position, head_size):
    half_size = head_size // 2
    freq_index = jnp.arange(half_size, dtype=jnp.float32)
    inverse = jnp.exp(freq_index * (-2.0 / head_size) * math.log(ROPE_BASE))
    angles = position.astype(jnp.float32)[:, None] * inverse[None, :]
    return (jnp.cos(angles), jnp.sin(angles))

def rotate(vectors, cosine, sine_part):
    half_size = vectors.shape[-1] // 2
    lower_half = vectors[..., :half_size]
    upper_half = vectors[..., half_size:]
    cosine = cosine[:, None, :]
    sine_part = sine_part[:, None, :]
    return jnp.concatenate([lower_half * cosine - upper_half * sine_part, upper_half * cosine + lower_half * sine_part], axis=-1)

def visible(segment, row_valid):
    row_index = jnp.arange(segment.shape[0], dtype=jnp.int32)
    same_seq = segment[:, None] == segment[None, :]
    return same_seq & (row_index[None, :] <= row_index[:, None]) & row_valid[:, None]

def attend(queries, key_vecs, values, allowed):
    row_count = queries.shape[0]
    factor = 1.0 / math.sqrt(HEAD)
    scores = low_back(jnp.einsum('qhgd,khd->hgqk', queries, key_vecs, precision=HIGHEST) * factor)
    row_peak = lax.optimization_barrier(jnp.max(jnp.where(allowed, scores, -1e+30), axis=-1, keepdims=True))
    raised = jnp.where(allowed, jnp.exp(jnp.where(allowed, scores - row_peak, 0.0)), 0.0)
    totals = lax.optimization_barrier(jnp.sum(raised, axis=-1, keepdims=True))
    attn_probs = raised / jnp.where(totals > 0, totals, 1.0)
    blended = jnp.einsum('hgqk,khd->qhgd', low(attn_probs), values, precision=HIGHEST)
    return blended.reshape(row_count, HEADS * HEAD)

def forward_pack(inputs, seq_lengths, first_gain, query_weight, key_weight, value_weight, output_weight, second_gain, gate_weight, up_weight, down_weight):
    row_count = inputs.shape[0]
    group_size = HEADS // KV_HEADS
    segment, position = pack_layout(seq_lengths, row_count)
    allowed = visible(segment, segment < SLOTS - 1)
    cosine, sine_part = rotary_tables(position, HEAD)
    first_scale = lax.rsqrt(lax.optimization_barrier(jnp.mean(inputs * inputs, axis=1, keepdims=True)) + EPSILON)
    normed_first = low(inputs * first_scale * first_gain)
    queries = low_back(matmul(normed_first, query_weight))
    key_vecs = low_back(matmul(normed_first, key_weight))
    values = low(low_back(matmul(normed_first, value_weight)))
    queries = low(rotate(queries.reshape(row_count, HEADS, HEAD), cosine, sine_part))
    key_vecs = low(rotate(key_vecs.reshape(row_count, KV_HEADS, HEAD), cosine, sine_part))
    blended = attend(queries.reshape(row_count, KV_HEADS, group_size, HEAD), key_vecs, values.reshape(row_count, KV_HEADS, HEAD), allowed)
    attended = low(low_back(blended))
    middle = inputs + low_back(matmul(attended, output_weight))
    second_scale = lax.rsqrt(lax.optimization_barrier(jnp.mean(middle * middle, axis=1, keepdims=True)) + EPSILON)
    normed_second = low(middle * second_scale * second_gain)
    gate_pre = low_back(matmul(normed_second, gate_weight))
    up_pre = low_back(matmul(normed_second, up_weight))
    hidden = low(jax.nn.silu(gate_pre) * up_pre)
    return middle + matmul(hidden, down_weight)

def reference(tokens, lengths, first_gain, query_weight, key_weight, value_weight, output_weight, second_gain, gate_weight, up_weight, down_weight, cotangent):
    weights = tuple((member.astype(jnp.float32) for member in (first_gain, query_weight, key_weight, value_weight, output_weight, second_gain, gate_weight, up_weight, down_weight)))
    pack_count = MB * PACKS
    inputs_all = tokens.astype(jnp.float32).reshape(pack_count, TOK_MB, D)
    seeds_all = cotangent.astype(jnp.float32).reshape(pack_count, TOK_MB, D)
    lengths_all = lengths.reshape(pack_count, SLOTS).astype(jnp.int32)

    def one_pack(running, packed):
        inputs, seed_grad, seq_lengths = packed

        def forward(inputs_in, *params):
            return forward_pack(inputs_in, seq_lengths, *params)
        result, pull_back = jax.vjp(forward, inputs, *weights)
        gradients = pull_back(seed_grad)
        running = tuple((earlier + gradient for earlier, gradient in zip(running, gradients[1:])))
        return (running, (result.astype(jnp.bfloat16), gradients[0]))
    initial = tuple((jnp.zeros(member.shape, jnp.float32) for member in weights))
    totals, (results, input_grads) = lax.scan(one_pack, initial, (inputs_all, seeds_all, lengths_all))
    layer_out = results.reshape(MB, PACKS * TOK_MB, D)
    input_grad = input_grads.reshape(MB, PACKS * TOK_MB, D)
    return (layer_out, input_grad, totals[0], totals[1], totals[2], totals[3], totals[4], totals[5], totals[6], totals[7], totals[8])
```

```python
import math

import jax
import jax.numpy as jnp
from jax import lax
from jax.sharding import PartitionSpec as P

HEADS = 16
KV_HEADS = 8
HEAD = 96
SLOTS = 6
GROUP = HEADS // KV_HEADS
LANES = 128

EPSILON = 1e-05
ROPE_BASE = 100000.0
NEG_LARGE = -1e30
AXES = ("dp", "tensor")
bf16 = jnp.bfloat16
f32 = jnp.float32


def pack_layout(seq_lengths, row_count):
    seq_ends = jnp.cumsum(seq_lengths)
    seq_starts = seq_ends - seq_lengths
    row_index = jnp.arange(row_count, dtype=jnp.int32)
    segment = jnp.sum((row_index[:, None] >= seq_ends[None, :]).astype(jnp.int32), axis=1)
    owner_hot = segment[:, None] == jnp.arange(seq_lengths.shape[0], dtype=jnp.int32)[None, :]
    position = row_index - jnp.sum(jnp.where(owner_hot, seq_starts[None, :], 0), axis=1)
    return (segment, position)


def rotary_tables(position, head_size):
    half_size = head_size // 2
    freq_index = jnp.arange(half_size, dtype=f32)
    inverse = jnp.exp(freq_index * (-2.0 / head_size) * math.log(ROPE_BASE))
    angles = position.astype(f32)[..., None] * inverse
    return (jnp.cos(angles), jnp.sin(angles))


def rotate(vectors, cosine, sine_part):
    half_size = vectors.shape[-1] // 2
    lower_half = vectors[..., :half_size]
    upper_half = vectors[..., half_size:]
    cosine = cosine[..., None, :]
    sine_part = sine_part[..., None, :]
    return jnp.concatenate(
        [
            lower_half * cosine - upper_half * sine_part,
            upper_half * cosine + lower_half * sine_part,
        ],
        axis=-1,
    )


def product(left_side, right_side):
    return jnp.dot(left_side, right_side, preferred_element_type=f32)


def across(left_side, right_side):
    return lax.dot_general(
        left_side, right_side, (((0,), (0,)), ((), ())), preferred_element_type=f32
    )


def against(left_side, right_side):
    return lax.dot_general(
        left_side, right_side, (((1,), (1,)), ((), ())), preferred_element_type=f32
    )


def bits_of(size):
    return [1 << k for k in range(size.bit_length() - 1)]


def near_first(size):
    masks = bits_of(size)
    return masks[:1] + masks[:0:-1]


def far_first(size):
    return bits_of(size)[::-1]


def rel_source(me, masks, block, count):
    place = jnp.arange(count, dtype=jnp.int32)
    step = place // block
    delta = jnp.zeros_like(step)
    for k, mask in enumerate(masks):
        delta = delta + ((step >> k) & 1) * mask
    return (me ^ delta) * block + place % block


def one_hot(source):
    count = source.shape[0]
    rows = lax.broadcasted_iota(jnp.int32, (count, count), 0)
    return (rows == source[None, :]).astype(bf16)


def join(parts):
    return parts[0] if len(parts) == 1 else jnp.concatenate(parts, axis=0)


def program(sizes):
    dp_n, tp_n = sizes["dp"], sizes["tensor"]
    world = dp_n * tp_n

    def swap(array, mask):
        return lax.ppermute(array, AXES, [(i, i ^ mask) for i in range(world)])

    def gather(own, masks, loose):
        held = [own]
        for k, mask in enumerate(masks):
            got = [swap(part, mask) for part in held]
            held = held + got
            if k < len(masks) - loose:
                held = [join(held)]
        return held

    def per_device(
        tokens,
        lengths,
        first_gain,
        query_weight,
        key_weight,
        value_weight,
        output_weight,
        second_gain,
        gate_weight,
        up_weight,
        down_weight,
        cotangent,
    ):
        micro, per_pack, width = tokens.shape
        rows = micro * per_pack
        qw, kw = query_weight.shape[1], key_weight.shape[1]
        ff = gate_weight.shape[1]
        wide = qw + 2 * kw
        shard = query_weight.shape[0]
        dp_i, t_i = lax.axis_index("dp"), lax.axis_index("tensor")
        me = dp_i * tp_n + t_i

        dp_attn = [m * tp_n for m in near_first(dp_n)]
        t_bits = bits_of(tp_n)[::-1]
        attn_masks = dp_attn + t_bits
        mlp_masks = [m * tp_n for m in far_first(dp_n)]

        x_low = tokens.reshape(rows, width)
        dy_low = cotangent.reshape(rows, width)

        gains = jnp.pad(
            jnp.stack([first_gain, second_gain], axis=1), ((0, 0), (0, LANES - 2))
        )
        own_qkv = jnp.concatenate([query_weight, key_weight, value_weight, gains], axis=1)
        own_gu = jnp.concatenate([gate_weight, up_weight], axis=1)
        own_down = down_weight.T

        def gather_attn(own):
            held = gather(own, dp_attn, 2)
            far = [swap(part, t_bits[0]) for part in held]
            pieces = [join(held), join(far)]
            for mask in t_bits[1:]:
                pieces = pieces + [swap(part, mask) for part in pieces]
            return pieces

        qkv_pieces = gather_attn(own_qkv)
        out_pieces = gather_attn(output_weight)
        gu_full = join(gather(own_gu, mlp_masks, 3))
        down_full = join(gather(own_down, mlp_masks, 3))
        n_pieces = len(qkv_pieces)
        part = width // n_pieces

        pick_attn = one_hot(rel_source(me, attn_masks, shard, width))
        mlp_source = rel_source(dp_i, [m // tp_n for m in mlp_masks], shard * tp_n, width)
        pick_mlp = one_hot(mlp_source)

        def order(array, pick):
            return product(array, pick).astype(bf16)

        def restore(array, pick):
            return against(array, pick)

        gains_rel = jnp.concatenate([piece[:, wide : wide + 2] for piece in qkv_pieces], axis=0)
        g1_rel = gains_rel[:, 0].astype(f32)
        g2 = restore(gains_rel[:, 1][None, :], pick_attn)[0]

        segment, position = jax.vmap(lambda own: pack_layout(own, per_pack))(lengths[:, 0])
        cosine, sine_part = rotary_tables(position, HEAD)
        row_index = jnp.arange(per_pack, dtype=jnp.int32)
        allowed = (
            (segment[:, :, None] == segment[:, None, :])
            & (row_index[None, None, :] <= row_index[None, :, None])
            & (segment < SLOTS - 1)[:, :, None]
        )[:, None, None]
        factor = 1.0 / math.sqrt(HEAD)

        inputs = x_low.astype(f32)
        r1 = lax.rsqrt(jnp.mean(inputs * inputs, axis=1, keepdims=True) + EPSILON)
        x_rel = order(x_low, pick_attn).astype(f32)
        n1_rel = (x_rel * r1 * g1_rel).astype(bf16)
        n1_parts = [n1_rel[:, k * part : (k + 1) * part] for k in range(n_pieces)]
        qkv = sum(product(a, b) for a, b in zip(n1_parts, qkv_pieces))
        shape = (micro, per_pack)
        queries = rotate(qkv[:, :qw].reshape(shape + (HEADS, HEAD)), cosine, sine_part)
        queries = queries.astype(bf16).reshape(shape + (KV_HEADS, GROUP, HEAD))
        keys = rotate(
            qkv[:, qw : qw + kw].reshape(shape + (KV_HEADS, HEAD)), cosine, sine_part
        ).astype(bf16)
        values = qkv[:, qw + kw : wide].astype(bf16).reshape(shape + (KV_HEADS, HEAD))
        scores = (
            jnp.einsum("pqhgd,pkhd->phgqk", queries, keys, preferred_element_type=f32) * factor
        )
        row_peak = jnp.max(jnp.where(allowed, scores, NEG_LARGE), axis=-1, keepdims=True)
        raised = jnp.where(allowed, jnp.exp(jnp.where(allowed, scores - row_peak, 0.0)), 0.0)
        totals = jnp.sum(raised, axis=-1, keepdims=True)
        probs = raised / jnp.where(totals > 0, totals, 1.0)
        probs_low = probs.astype(bf16)
        attended = jnp.einsum("phgqk,pkhd->pqhgd", probs_low, values, preferred_element_type=f32)
        attended = attended.reshape(rows, qw).astype(bf16)
        att_rel = order(attended, pick_attn)
        att_parts = [att_rel[:, k * part : (k + 1) * part] for k in range(n_pieces)]
        middle = inputs + sum(product(a, b) for a, b in zip(att_parts, out_pieces))
        r2 = lax.rsqrt(jnp.mean(middle * middle, axis=1, keepdims=True) + EPSILON)
        n2 = (middle * r2 * g2).astype(bf16)
        n2_rel = order(n2, pick_mlp)
        dy_rel = order(dy_low, pick_mlp)

        def spread(own):
            return join(gather(own, t_bits, tp_n))

        def collect(partial):
            for mask in t_bits[::-1]:
                half = partial.shape[0] // 2
                got = swap(partial[half:].astype(bf16), mask)
                partial = partial[:half].astype(f32) + got.astype(f32)
            return partial

        dy_all = spread(dy_rel)
        n2_all = spread(n2_rel)
        gu = product(n2_all, gu_full)
        gate, up = gu[:, :ff], gu[:, ff:]
        sig = jax.nn.sigmoid(gate)
        hidden = (gate * sig * up).astype(bf16)
        dhid = product(dy_all, down_full)
        dgate = (dhid * up * sig * (1.0 + gate * (1.0 - sig))).astype(bf16)
        dup = (dhid * gate * sig).astype(bf16)
        dgu = jnp.concatenate([dgate, dup], axis=1)
        dn2 = restore(collect(against(dgu, gu_full).astype(bf16)).astype(bf16), pick_mlp)
        down_sum = collect(against(hidden, down_full).astype(bf16)).astype(bf16)
        layer_out = (middle + restore(down_sum, pick_mlp)).astype(bf16)

        def reduce_rows(own_half, sent_half, masks):
            total = own_half() + swap(sent_half().astype(bf16), masks[0]).astype(f32)
            for mask in masks[1:]:
                half = total.shape[0] // 2
                got = swap(total[half:].astype(bf16), mask)
                total = total[:half] + got.astype(f32)
            return total

        half = width // 2

        def mlp_grad(left, right):
            return reduce_rows(
                lambda: across(left[:, :half], right),
                lambda: across(left[:, half:], right),
                mlp_masks[::-1],
            )

        down_grad = mlp_grad(dy_all, hidden).T
        gate_grad = mlp_grad(n2_all, dgate)
        up_grad = mlp_grad(n2_all, dup)

        dy = dy_low.astype(f32)
        weighted = dn2 * g2
        dmid = dy + r2 * weighted - middle * (r2 * r2 * r2) * jnp.mean(
            weighted * middle, axis=1, keepdims=True
        )
        dmb = dmid.astype(bf16)

        def attn_grad(lefts, right):
            held = [across(left, right) for left in lefts]
            for mask in t_bits[1:][::-1]:
                n = len(held) // 2
                got = [swap(piece.astype(bf16), mask) for piece in held[n:]]
                held = [a + b.astype(f32) for a, b in zip(held[:n], got)]
            return reduce_rows(
                lambda: held[0], lambda: held[1], [t_bits[0]] + dp_attn[::-1]
            )

        output_grad = attn_grad(att_parts, dmb)
        datt_rel = jnp.concatenate([against(dmb, piece) for piece in out_pieces], axis=1)
        datt = restore(datt_rel.astype(bf16), pick_attn).astype(bf16)
        datt = datt.reshape(shape + (KV_HEADS, GROUP, HEAD))
        dprob = jnp.einsum("pqhgd,pkhd->phgqk", datt, values, preferred_element_type=f32)
        delta = jnp.sum(probs * dprob, axis=-1, keepdims=True)
        dscore = (probs * (dprob - delta)).astype(bf16)
        dvalue = jnp.einsum("phgqk,pqhgd->pkhd", probs_low, datt, preferred_element_type=f32)
        dqr = jnp.einsum("phgqk,pkhd->pqhgd", dscore, keys, preferred_element_type=f32) * factor
        dkr = jnp.einsum("phgqk,pqhgd->pkhd", dscore, queries, preferred_element_type=f32) * factor
        dq = rotate(dqr.reshape(shape + (HEADS, HEAD)), cosine, -sine_part)
        dk = rotate(dkr, cosine, -sine_part)
        dqkv = jnp.concatenate(
            [
                dq.astype(bf16).reshape(rows, qw),
                dk.astype(bf16).reshape(rows, kw),
                dvalue.astype(bf16).reshape(rows, kw),
            ],
            axis=1,
        )
        qkv_grad = attn_grad(n1_parts, dqkv)
        dn1_rel = jnp.concatenate(
            [against(dqkv, piece[:, :wide]) for piece in qkv_pieces], axis=1
        )
        weighted = dn1_rel * g1_rel
        part_rel = r1 * weighted - x_rel * (r1 * r1 * r1) * jnp.mean(
            weighted * x_rel, axis=1, keepdims=True
        )
        high = part_rel.astype(bf16)
        low = (part_rel - high.astype(f32)).astype(bf16)
        input_grad = dmid + restore(high, pick_attn) + restore(low, pick_attn)

        own_wide = own_qkv[:, :wide].astype(f32)
        first_gain_grad = jnp.sum(own_wide * qkv_grad, axis=1) / first_gain.astype(f32)
        second = jnp.sum(
            gate_weight.astype(f32) * gate_grad + up_weight.astype(f32) * up_grad, axis=1
        )
        second = lax.psum(second, "tensor")
        second = lax.dynamic_slice(second, (t_i * shard,), (shard,))
        second_gain_grad = second / second_gain.astype(f32)

        return (
            layer_out.reshape(tokens.shape),
            input_grad.reshape(tokens.shape),
            first_gain_grad,
            qkv_grad[:, :qw],
            qkv_grad[:, qw : qw + kw],
            qkv_grad[:, qw + kw :],
            output_grad,
            second_gain_grad,
            gate_grad,
            up_grad,
            down_grad,
        )

    return per_device


def solution(mesh):
    rows = P(None, AXES, None)
    split = P(AXES, None)
    placed = (
        rows,
        rows,
        P(AXES),
        split,
        split,
        split,
        split,
        P(AXES),
        P("dp", "tensor"),
        P("dp", "tensor"),
        P("tensor", "dp"),
        rows,
    )
    return jax.shard_map(
        program(dict(mesh.shape)),
        mesh=mesh,
        in_specs=placed,
        out_specs=(
            rows,
            rows,
            P(AXES),
            split,
            split,
            split,
            split,
            P(AXES),
            P("dp", "tensor"),
            P("dp", "tensor"),
            P("tensor", "dp"),
        ),
        check_vma=False,
    )
```

```python
import functools
import math

import jax
import jax.numpy as jnp
from jax import lax
from jax.experimental import pallas as pl
from jax.experimental.pallas import tpu as pltpu
from jax.sharding import PartitionSpec as P

HEADS = 16
KV_HEADS = 8
HEAD = 96
SLOTS = 6
GROUP = HEADS // KV_HEADS
LANES = 128

EPSILON = 1e-05
ROPE_BASE = 100000.0
NEG_LARGE = -1e30
AXES = ("dp", "tensor")
bf16 = jnp.bfloat16
f32 = jnp.float32


def pack_layout(seq_lengths, row_count):
    seq_ends = jnp.cumsum(seq_lengths)
    seq_starts = seq_ends - seq_lengths
    row_index = jnp.arange(row_count, dtype=jnp.int32)
    segment = jnp.sum((row_index[:, None] >= seq_ends[None, :]).astype(jnp.int32), axis=1)
    owner_hot = segment[:, None] == jnp.arange(seq_lengths.shape[0], dtype=jnp.int32)[None, :]
    position = row_index - jnp.sum(jnp.where(owner_hot, seq_starts[None, :], 0), axis=1)
    return (segment, position)


def rotary_tables(position, head_size):
    half_size = head_size // 2
    freq_index = jnp.arange(half_size, dtype=f32)
    inverse = jnp.exp(freq_index * (-2.0 / head_size) * math.log(ROPE_BASE))
    angles = position.astype(f32)[..., None] * inverse
    return (jnp.cos(angles), jnp.sin(angles))


def product(left_side, right_side):
    return jnp.dot(left_side, right_side, preferred_element_type=f32)


def across(left_side, right_side):
    return lax.dot_general(
        left_side, right_side, (((0,), (0,)), ((), ())), preferred_element_type=f32
    )


def against(left_side, right_side):
    return lax.dot_general(
        left_side, right_side, (((1,), (1,)), ((), ())), preferred_element_type=f32
    )


def bits_of(size):
    return [1 << k for k in range(size.bit_length() - 1)]


def rel_source(me, masks, block, count):
    place = jnp.arange(count, dtype=jnp.int32)
    step = place // block
    delta = jnp.zeros_like(step)
    for k, mask in enumerate(masks):
        delta = delta + ((step >> k) & 1) * mask
    return (me ^ delta) * block + place % block


def one_hot(source):
    count = source.shape[0]
    rows = lax.broadcasted_iota(jnp.int32, (count, count), 0)
    return (rows == source[None, :]).astype(bf16)


def join(parts):
    return parts[0] if len(parts) == 1 else jnp.concatenate(parts, axis=0)


BAND = 4 * HEAD


def turn(array, cosine, sine_part):
    lane = lax.broadcasted_iota(jnp.int32, array.shape, 1)
    swapped = jnp.where(
        lane % HEAD < HEAD // 2,
        pltpu.roll(array, BAND - HEAD // 2, 1),
        pltpu.roll(array, HEAD // 2, 1),
    )
    return array * cosine + swapped * sine_part


def head_masks():
    lane = lax.broadcasted_iota(jnp.int32, (1, BAND), 1)
    return [jnp.where(lane // HEAD == h, 1.0, 0.0) for h in range(4)]


def stack_heads(bands, masks):
    return jnp.concatenate([band * mask.astype(bf16) for band in bands for mask in masks], axis=0)


def unstack_heads(stacked, masks, per_pack):
    found = []
    for g in range(GROUP):
        total = 0.0
        for h in range(4):
            first = (g * 4 + h) * per_pack
            total = total + stacked[first : first + per_pack] * masks[h]
        found.append(total)
    return found


def pack_probs(stacked, keys, allowed):
    per_pack = keys.shape[0]
    scores = against(stacked, keys) * (1.0 / math.sqrt(HEAD))
    scores = scores.reshape(-1, per_pack, per_pack)
    peak = jnp.max(jnp.where(allowed, scores, NEG_LARGE), axis=-1, keepdims=True)
    raised = jnp.where(allowed, jnp.exp(jnp.where(allowed, scores - peak, 0.0)), 0.0)
    totals = jnp.sum(raised, axis=-1, keepdims=True)
    return raised / jnp.where(totals > 0, totals, 1.0)


def columns(band):
    return pl.ds(band * BAND, BAND)


def piece_rows(pieces, place, mixed):
    if not mixed:
        return jnp.concatenate([piece[:, place] for piece in pieces], axis=0)
    n = pieces[0].shape[0] // 2
    found = []
    for a, b in (pieces[:2], pieces[2:]):
        for k in (slice(0, n), slice(n, 2 * n)):
            found += [a[k, place], b[k, place]]
    return jnp.concatenate(found, axis=0)


def forward_kernel(micro, per_pack, kv_bands, *refs):
    x_ref, cos_ref, sin_ref, mask_ref, *piece_refs = refs[:-4]
    qkv_ref, att_ref, n1_ref, gains_ref = refs[-4:]
    q_bands = GROUP * kv_bands
    q_refs, kv_refs = piece_refs[:4], piece_refs[4:]
    tail = pl.ds(2 * kv_bands * BAND, LANES)
    gains = jnp.transpose(piece_rows(kv_refs, tail, False).astype(f32))
    gains_ref[...] = gains[: gains_ref.shape[0]]
    inputs = x_ref[...].astype(f32)
    scale = lax.rsqrt(jnp.mean(inputs * inputs, axis=1, keepdims=True) + EPSILON)
    n1_ref[...] = (inputs * scale * gains[:1]).astype(bf16)
    for band in range(q_bands + 2 * kv_bands):
        in_q = band < q_bands
        place = columns(band if in_q else band - q_bands)
        total = product(n1_ref[...], piece_rows(q_refs if in_q else kv_refs, place, in_q))
        if band < q_bands + kv_bands:
            total = turn(total, cos_ref[...], sin_ref[...])
        qkv_ref[:, columns(band)] = total.astype(bf16)

    masks = head_masks()

    def one_pack(pack, carry):
        rows = pl.ds(pl.multiple_of(pack * per_pack, per_pack), per_pack)
        allowed = (mask_ref[pl.ds(pack, 1)] > 0.0)
        for j in range(kv_bands):
            bands = [g * kv_bands + j for g in range(GROUP)]
            stacked = stack_heads([qkv_ref[rows, columns(b)] for b in bands], masks)
            keys = qkv_ref[rows, columns(q_bands + j)]
            values = qkv_ref[rows, columns(q_bands + kv_bands + j)]
            probs = pack_probs(stacked, keys, allowed)
            mixed = product(probs.astype(bf16).reshape(-1, per_pack), values)
            for b, band in zip(bands, unstack_heads(mixed, masks, per_pack)):
                att_ref[rows, columns(b)] = band.astype(bf16)
        return carry

    lax.fori_loop(0, micro, one_pack, 0)


def pack_kernel(q_ref, k_ref, v_ref, gains_ref, o_ref, out_ref):
    heads = [
        q_ref[:, (k * GROUP + g) * HEAD : (k * GROUP + g + 1) * HEAD]
        for g in range(GROUP)
        for k in range(KV_HEADS)
    ]
    first = 0
    for piece in (
        jnp.concatenate(heads, axis=1), k_ref[...], v_ref[...], gains_ref[...], o_ref[...]
    ):
        out_ref[:, first : first + piece.shape[1]] = piece
        first += piece.shape[1]


def backward_kernel(micro, per_pack, kv_bands, *refs):
    dmb_ref, qkv_ref, cos_ref, sin_ref, mask_ref, pick_ref, *out_refs = refs[:8]
    dqkv_ref, datt_ref = refs[-2:]
    half = pick_ref.shape[1] // 2
    datt = 0.0
    for k, piece in enumerate(out_refs):
        part = against(dmb_ref[...], piece[...]).astype(bf16)
        datt = datt + against(part, pick_ref[:, k * half : (k + 1) * half])
    datt_ref[...] = datt.astype(bf16)
    q_bands = GROUP * kv_bands
    factor = 1.0 / math.sqrt(HEAD)
    masks = head_masks()

    def one_pack(pack, carry):
        rows = pl.ds(pl.multiple_of(pack * per_pack, per_pack), per_pack)
        allowed = (mask_ref[pl.ds(pack, 1)] > 0.0)
        cosine, sine_part = cos_ref[rows, :], -sin_ref[rows, :]
        for j in range(kv_bands):
            bands = [g * kv_bands + j for g in range(GROUP)]
            stacked = stack_heads([qkv_ref[rows, columns(b)] for b in bands], masks)
            keys = qkv_ref[rows, columns(q_bands + j)]
            values = qkv_ref[rows, columns(q_bands + kv_bands + j)]
            grads = stack_heads([datt_ref[rows, columns(b)] for b in bands], masks)
            probs = pack_probs(stacked, keys, allowed)
            dprob = against(grads, values).reshape(probs.shape)
            delta = jnp.sum(probs * dprob, axis=-1, keepdims=True)
            dscore = (probs * (dprob - delta)).astype(bf16).reshape(-1, per_pack)
            dvalue = across(probs.astype(bf16).reshape(-1, per_pack), grads)
            dkey = turn(across(dscore, stacked) * factor, cosine, sine_part)
            dquery = product(dscore, keys) * factor
            for b, band in zip(bands, unstack_heads(dquery, masks, per_pack)):
                dqkv_ref[rows, columns(b)] = turn(band, cosine, sine_part).astype(bf16)
            dqkv_ref[rows, columns(q_bands + j)] = dkey.astype(bf16)
            dqkv_ref[rows, columns(q_bands + kv_bands + j)] = dvalue.astype(bf16)
        return carry

    lax.fori_loop(0, micro, one_pack, 0)


def mlp_kernel(ff, *refs):
    n2_ref, dy_ref, gu_ref, down_ref = refs[:4]
    hidden_ref, dgu_ref, *dn2_refs = refs[-4:]
    both = product(n2_ref[...], gu_ref[...])
    gate, up = both[:, :ff], both[:, ff:]
    dhid = product(dy_ref[...], down_ref[...])
    sig = jax.nn.sigmoid(gate)
    passed = gate * sig
    hidden_ref[...] = (passed * up).astype(bf16)
    dgu_ref[:, :ff] = (dhid * up * sig * (1.0 + gate * (1.0 - sig))).astype(bf16)
    dgu_ref[:, ff:] = (dhid * passed).astype(bf16)
    dn2 = against(dgu_ref[...], gu_ref[...]).astype(bf16)
    put_by_step(dn2_refs, [dn2] * 2)


def put_by_step(refs, values):
    for k, (ref, value) in enumerate(zip(refs, values)):

        @pl.when(pl.program_id(0) == k)
        def _(ref=ref, value=value):
            ref[...] = value.astype(ref.dtype)


def shape_of(rows, columns, kind):
    return jax.ShapeDtypeStruct((rows, columns), kind)


def estimate(flops):
    return pl.CostEstimate(flops=100000000000, bytes_accessed=0, transcendentals=0)


LIMIT = pltpu.CompilerParams(vmem_limit_bytes=56 * 1024 * 1024)
ANYWHERE = pl.BlockSpec(memory_space=pl.ANY)


def fixed(rows, columns, row=0, column=0):
    return pl.BlockSpec((rows, columns), lambda i: (row, column))


def mlp_call(first, n2, dy, gu, down, *earlier):
    rows, width = n2.shape
    ff = down.shape[1]
    block = rows // 4

    def band(columns):
        return pl.BlockSpec((block, columns), lambda i: (first + i, 0))

    return pl.pallas_call(
        functools.partial(mlp_kernel, ff),
        grid=(2,),
        in_specs=[band(width), band(width), fixed(*gu.shape), fixed(*down.shape)]
        + [ANYWHERE] * len(earlier),
        out_specs=[band(ff), band(2 * ff), fixed(block, width), fixed(block, width)],
        out_shape=[shape_of(rows, ff, bf16), shape_of(rows, 2 * ff, bf16)]
        + [shape_of(block, width, bf16)] * 2,
        input_output_aliases={4 + k: k for k in range(len(earlier) - 1)},
        compiler_params=LIMIT,
        cost_estimate=estimate(10 * 2 * block * width * ff),
    )(n2, dy, gu, down, *earlier)


def sent_kernel(left_ref, right_ref, token_ref, out_ref):
    out_ref[...] = across(left_ref[...], right_ref[...]).astype(bf16)


def sent_call(left, right, at, columns, token):
    count, width = left.shape
    block = width // 4
    return pl.pallas_call(
        sent_kernel,
        grid=(2,),
        in_specs=[
            pl.BlockSpec((count, block), lambda i: (0, 2 + i)),
            fixed(count, columns, 0, at // columns),
            ANYWHERE,
        ],
        out_specs=pl.BlockSpec((block, columns), lambda i: (i, 0)),
        out_shape=shape_of(2 * block, columns, bf16),
        compiler_params=LIMIT,
        cost_estimate=estimate(4 * count * block * columns),
    )(left, right, token)


def kept_kernel(left_ref, right_ref, got_ref, token_ref, keep_ref, send_ref):
    total = across(left_ref[...], right_ref[...]) + got_ref[...].astype(f32)
    put_by_step((keep_ref, send_ref), (total, total))


def kept_call(left, right, at, columns, got, token):
    count, width = left.shape
    block = width // 4
    return pl.pallas_call(
        kept_kernel,
        grid=(2,),
        in_specs=[
            pl.BlockSpec((count, block), lambda i: (0, i)),
            fixed(count, columns, 0, at // columns),
            pl.BlockSpec((block, columns), lambda i: (i, 0)),
            ANYWHERE,
        ],
        out_specs=[fixed(block, columns)] * 2,
        out_shape=[shape_of(block, columns, f32), shape_of(block, columns, bf16)],
        compiler_params=LIMIT,
        cost_estimate=estimate(4 * count * block * columns),
    )(left, right, got, token)


def sum_kernel(count, *refs):
    total = 0.0
    for ref in refs[:count]:
        total = total + ref[...].astype(f32)
    outs = refs[count + 1 :]
    rows = total.shape[0] // len(outs)
    for k, out in enumerate(outs):
        out[...] = total[k * rows : (k + 1) * rows].astype(out.dtype)


def sum_call(arrays, kinds, token):
    rows, columns = arrays[0].shape
    block = columns // 2 if columns % 256 == 0 else columns
    part = rows // len(kinds)
    return pl.pallas_call(
        functools.partial(sum_kernel, len(arrays)),
        grid=(columns // block,),
        in_specs=[pl.BlockSpec((rows, block), lambda i: (0, i))] * len(arrays) + [ANYWHERE],
        out_specs=[pl.BlockSpec((part, block), lambda i: (0, i))] * len(kinds),
        out_shape=[shape_of(part, columns, kind) for kind in kinds],
        compiler_params=LIMIT,
        cost_estimate=estimate(rows * columns),
    )(*arrays, token)


def norm_back(upstream, signal, gain):
    inverse = lax.rsqrt(jnp.mean(signal * signal, axis=1, keepdims=True) + EPSILON)
    weighted = upstream * gain
    mixed = jnp.mean(weighted * signal, axis=1, keepdims=True)
    return inverse * weighted - signal * (inverse * inverse * inverse) * mixed


def second_norm_kernel(*refs):
    near_ref, core_ref, x_ref, pick_ref, dy_ref, middle_ref, gain_ref, _ = refs[:8]
    dmid_ref, dmb_ref = refs[8:]
    dn2 = near_ref[...].astype(f32) + core_ref[...].astype(f32) + x_ref[...].astype(f32)
    dn2 = against(dn2.astype(bf16), pick_ref[...])
    dmid = dy_ref[...].astype(f32) + norm_back(dn2, middle_ref[...], gain_ref[...])
    dmid_ref[...] = dmid
    dmb_ref[...] = dmid.astype(bf16)


def first_norm_kernel(band, *refs):
    dqkv_ref, x_ref, gains_ref, pick_ref, dmid_ref, *piece_refs = refs[:-2]
    out_ref = refs[-1]
    dn1 = 0.0
    bands = dqkv_ref.shape[1] // band
    for k in range(bands):
        in_q = k < bands // 2
        place = pl.ds((k if in_q else k - bands // 2) * band, band)
        found = piece_rows(piece_refs[:4] if in_q else piece_refs[4:], place, in_q)
        dn1 = dn1 + against(dqkv_ref[:, pl.ds(k * band, band)], found)
    part = norm_back(dn1, x_ref[...].astype(f32), gains_ref[:1])
    high = part.astype(bf16)
    low = (part - high.astype(f32)).astype(bf16)
    out_ref[...] = dmid_ref[...] + against(high, pick_ref[...]) + against(low, pick_ref[...])


def down_kernel(hidden_ref, down_ref, token_ref, *out_refs):
    rows = against(hidden_ref[...], down_ref[...])
    put_by_step(out_refs, [rows] * 4)


def down_call(hidden, down, token):
    rows, ff = hidden.shape
    width, block = down.shape[0], hidden.shape[0] // 4
    return pl.pallas_call(
        down_kernel,
        grid=(4,),
        in_specs=[pl.BlockSpec((block, ff), lambda i: (i, 0)), fixed(width, ff), ANYWHERE],
        out_specs=[fixed(block, width)] * 4,
        out_shape=[shape_of(block, width, bf16)] * 4,
        compiler_params=LIMIT,
        cost_estimate=estimate(2 * rows * width * ff),
    )(hidden, down, token)


def layer_kernel(own_ref, core_ref, x_ref, pick_ref, middle_ref, token_ref, out_ref):
    total = own_ref[...].astype(f32) + core_ref[...].astype(f32) + x_ref[...].astype(f32)
    total = middle_ref[...] + against(total.astype(bf16), pick_ref[...])
    out_ref[...] = total.astype(bf16)


def kernel_call(body, outs, cost, *args, token=None, scratch=()):
    tokens = () if token is None else (token,)
    return pl.pallas_call(
        body,
        out_shape=outs,
        in_specs=[pl.BlockSpec(memory_space=pltpu.VMEM)] * len(args) + [ANYWHERE] * len(tokens),
        out_specs=[pl.BlockSpec(memory_space=pltpu.VMEM)] * len(outs),
        scratch_shapes=list(scratch),
        compiler_params=LIMIT,
        cost_estimate=cost,
    )(*args, *tokens)


def after(array, *others):
    return lax.optimization_barrier((array,) + others)[0]


def together(*arrays):
    return lax.optimization_barrier(arrays)


def program(sizes):
    dp_n, tp_n = sizes["dp"], sizes["tensor"]
    world = dp_n * tp_n

    def swap(array, mask):
        return lax.ppermute(array, AXES, [(i, i ^ mask) for i in range(world)])

    dp_bits = [m * tp_n for m in bits_of(dp_n)]
    y_mask, z_masks = dp_bits[0], dp_bits[:0:-1]
    t_masks = bits_of(tp_n)[::-1]
    x_mask, core_mask = t_masks
    attn_masks = z_masks + [y_mask, x_mask, core_mask]
    mlp_masks = z_masks + [y_mask]

    def gather_far(own):
        if len(z_masks) == 2:
            one, two = z_masks
            return [own, swap(own, one), swap(own, two), swap(own, one ^ two)]
        held = own
        for mask in z_masks:
            held = join([held, swap(held, mask)])
        return [held]

    def finish(pair, token):
        (total,) = sum_call(pair, [f32], token)
        for mask in z_masks[:-2][::-1]:
            n = total.shape[0] // 2
            total = total[:n] + swap(total[n:].astype(bf16), mask).astype(f32)
        return total

    def per_device(
        tokens,
        lengths,
        first_gain,
        query_weight,
        key_weight,
        value_weight,
        output_weight,
        second_gain,
        gate_weight,
        up_weight,
        down_weight,
        cotangent,
    ):
        micro, per_pack, width = tokens.shape
        rows = micro * per_pack
        qw, kw = query_weight.shape[1], key_weight.shape[1]
        ff = gate_weight.shape[1]
        wide = qw + 2 * kw
        shard = query_weight.shape[0]
        dp_i, t_i = lax.axis_index("dp"), lax.axis_index("tensor")
        me = dp_i * tp_n + t_i

        x_low = tokens.reshape(rows, width)
        dy_low = cotangent.reshape(rows, width)
        half, quarter = width // 2, width // 4

        gains = jnp.pad(
            jnp.stack([first_gain, second_gain], axis=1), ((0, 0), (0, LANES - 2))
        )
        (own_attn,) = kernel_call(
            pack_kernel,
            [jax.ShapeDtypeStruct((shard, 2 * qw + 2 * kw + LANES), bf16)],
            None,
            query_weight,
            key_weight,
            value_weight,
            gains,
            output_weight,
        )
        own_gu = jnp.concatenate([gate_weight, up_weight], axis=1)
        own_down = down_weight.T
        own_mlp = jnp.concatenate([own_gu, own_down], axis=1)

        attn_source = rel_source(me, attn_masks, shard, width)
        pick_attn = one_hot(attn_source)
        head, lane = attn_source // HEAD, attn_source % HEAD
        pick_out = one_hot((head % GROUP * KV_HEADS + head // GROUP) * HEAD + lane)
        pick_mlp = one_hot(
            rel_source(dp_i, [m // tp_n for m in mlp_masks], shard * tp_n, width)
        )

        def order(array, pick):
            return product(array, pick).astype(bf16)

        def restore(array, pick):
            return against(array, pick)

        def middle_swap(array):
            n = array.shape[0] // 4
            return join([array[:n], array[2 * n : 3 * n], array[n : 2 * n], array[3 * n :]])

        dy_rel = order(after(dy_low, own_attn), pick_mlp)
        *far, mlp_y, dy_x = together(
            *gather_far(own_attn), swap(own_mlp, y_mask), swap(dy_rel, x_mask)
        )
        cut_q, cut_kv = slice(0, qw), slice(qw, qw + 2 * kw + LANES)
        edge = cut_kv.stop + width // 2
        cut_left, cut_right = slice(cut_kv.stop, edge), slice(edge, None)
        q_four, kv_four, left_four, right_four = [
            join([piece[:, cut] for piece in far]) for cut in (cut_q, cut_kv, cut_left, cut_right)
        ]

        q_x, kv_y, left_x, right_y, down_z = together(
            swap(q_four, x_mask),
            swap(kv_four, y_mask),
            swap(left_four, x_mask),
            swap(right_four, y_mask),
            swap(after(own_down, q_four), z_masks[0]),
        )
        q_eight = join([q_four, q_x])
        kv_eight = join([kv_four, kv_y])

        q_y, kv_x, q_c, kv_c, gu_z = together(
            swap(q_eight, y_mask),
            swap(kv_eight, x_mask),
            swap(q_eight, core_mask),
            swap(kv_eight, core_mask),
            swap(after(own_gu, q_x), z_masks[0]),
        )

        left_eight = join([left_four, left_x])
        right_eight = join([right_four, right_y])
        left_y = swap(after(left_eight, q_y), y_mask)
        right_x = swap(after(right_eight, q_y), x_mask)
        q_yc, kv_xc = together(swap(q_y, core_mask), swap(kv_x, core_mask))
        q_pieces = [q_eight, q_y, q_c, q_yc]
        kv_pieces = [kv_eight, kv_x, kv_c, kv_xc]

        def next_far(own, first):
            held, came = join([own, first]), [first]
            for mask in z_masks[1:]:
                came.append(swap(held, mask))
                held = join([held, came[-1]])
            return held, came

        gu_near, gu_came = next_far(own_gu, gu_z)
        gu_y1 = swap(gu_z, y_mask)
        down_y1 = swap(down_z, y_mask)

        segment, position = jax.vmap(lambda own: pack_layout(own, per_pack))(lengths[:, 0])
        cosine, sine_part = rotary_tables(position, HEAD)
        row_index = jnp.arange(per_pack, dtype=jnp.int32)
        allowed = (
            (segment[:, :, None] == segment[:, None, :])
            & (row_index[None, None, :] <= row_index[None, :, None])
            & (segment < SLOTS - 1)[:, :, None]
        ).astype(f32)

        inputs = x_low.astype(f32)
        r1 = lax.rsqrt(jnp.mean(inputs * inputs, axis=1, keepdims=True) + EPSILON)
        x_rel = order(x_low, pick_attn)
        half_tables = (cosine.reshape(rows, -1), sine_part.reshape(rows, -1))
        cos_band = jnp.tile(half_tables[0], (1, BAND // half_tables[0].shape[1]))
        sin_band = jnp.tile(jnp.concatenate([-half_tables[1], half_tables[1]], axis=1), (1, 4))
        kv_bands = kw // BAND
        shapes = (micro, per_pack, kv_bands)
        cost = pl.CostEstimate(
            flops=100000000000, bytes_accessed=0, transcendentals=0
        )
        qkv, attended, n1_rel, gains_rel = kernel_call(
            functools.partial(forward_kernel, *shapes),
            [
                jax.ShapeDtypeStruct((rows, wide), bf16),
                jax.ShapeDtypeStruct((rows, qw), bf16),
                jax.ShapeDtypeStruct((rows, width), bf16),
                jax.ShapeDtypeStruct((8, width), f32),
            ],
            cost,
            x_rel,
            cos_band,
            sin_band,
            allowed,
            *q_pieces,
            *kv_pieces,
        )
        g1_rel = gains_rel[:1]
        g2 = restore(gains_rel[1:2].astype(bf16), pick_attn)
        n1_parts = [n1_rel[:, :half], n1_rel[:, half:]]

        left_16 = middle_swap(join([left_eight, left_y]))
        right_16 = join([right_eight, right_x])
        out_16 = jnp.concatenate([left_16, right_16], axis=1)
        out_pieces = [out_16, swap(out_16, core_mask)]
        dy_near = join([dy_rel, dy_x])
        dy_c = swap(after(dy_near, attended), core_mask)

        att_rel = order(attended, pick_out)
        att_parts = [att_rel[:, :half], att_rel[:, half:]]
        middle = inputs + sum(product(a, b) for a, b in zip(att_parts, out_pieces))
        r2 = lax.rsqrt(jnp.mean(middle * middle, axis=1, keepdims=True) + EPSILON)
        n2 = (middle * r2 * g2).astype(bf16)

        n2_rel = after(order(n2, pick_mlp), *gu_came, gu_y1, down_y1)
        n2_x = swap(n2_rel, x_mask)
        n2_c = swap(n2_rel, core_mask)
        down_near, down_came = next_far(own_down, after(down_z, n2_rel))
        gu_full = join(
            [gu_near, mlp_y[:, : 2 * ff], gu_y1] + [swap(a, y_mask) for a in gu_came[1:]]
        )
        down_full = join(
            [down_near, mlp_y[:, 2 * ff :], down_y1] + [swap(a, y_mask) for a in down_came[1:]]
        )
        n2_all = join([n2_rel, n2_c, n2_x, swap(n2_x, core_mask)])
        dy_all = join([dy_rel, dy_c[:rows], dy_x, dy_c[rows:]])

        *grown, far_own, far_send = mlp_call(2, n2_all, dy_all, gu_full, down_full, n2_all)
        far_c = swap(far_send, core_mask)
        (dn2_sum,) = sum_call([far_own, far_c], [bf16], far_own)
        dn2_x = swap(dn2_sum, x_mask)
        hidden, dgu, near_own, near_send = mlp_call(
            0, n2_all, dy_all, gu_full, down_full, *grown, dn2_sum
        )
        near_c = swap(near_send, core_mask)
        down_b = sent_call(dy_all, hidden, 0, ff, near_own)
        down_got = swap(down_b, y_mask)

        dmid, dmb = kernel_call(
            second_norm_kernel,
            [shape_of(rows, width, f32), shape_of(rows, width, bf16)],
            estimate(4 * rows * width * width),
            near_own,
            near_c,
            dn2_x,
            pick_mlp,
            dy_low,
            middle,
            g2,
            token=down_b,
        )
        og_b = sent_call(att_rel, dmb, 0, width, dmb)
        og_c = swap(og_b, core_mask)
        gate_b = sent_call(n2_all, dgu, 0, ff, og_b)
        gate_got = swap(gate_b, y_mask)
        og = kept_call(att_rel, dmb, 0, width, og_c, gate_b)
        og_x = swap(og[1], x_mask)
        (dqkv,) = kernel_call(
            functools.partial(backward_kernel, *shapes),
            [shape_of(rows, wide, bf16)],
            cost,
            dmb,
            qkv,
            cos_band,
            sin_band,
            allowed,
            pick_out,
            *out_pieces,
            token=og[0],
            scratch=[pltpu.VMEM((rows, qw), bf16)],
        )
        qkv_b = sent_call(n1_rel, dqkv, 0, wide, dqkv)
        qkv_c = swap(qkv_b, core_mask)
        far_mask, near_mask = z_masks[-1], z_masks[-2]
        step = [f32, bf16]

        def onward(pair, got, mask, token):
            pair = sum_call([pair[0], got], step, token)
            return pair, swap(pair[1], mask)

        down_k = kept_call(dy_all, hidden, 0, ff, down_got, qkv_b)
        down_got = swap(down_k[1], far_mask)
        qkv_k = kept_call(n1_rel, dqkv, 0, wide, qkv_c, down_k[0])
        qkv_got = swap(qkv_k[1], x_mask)
        og, og_got = onward(og, og_x, y_mask, qkv_k[0])
        (input_grad,) = kernel_call(
            functools.partial(first_norm_kernel, 2 * BAND),
            [shape_of(rows, width, f32)],
            estimate(2 * rows * width * (wide + 2 * width)),
            dqkv,
            x_rel,
            gains_rel,
            pick_attn,
            dmid,
            *q_pieces,
            *kv_pieces,
            token=og[0],
        )
        down_k, down_got = onward(down_k, down_got, near_mask, input_grad)
        up_b = sent_call(n2_all, dgu, ff, ff, down_k[0])
        up_got = swap(up_b, y_mask)
        gate_k = kept_call(n2_all, dgu, 0, ff, gate_got, up_b)
        gate_got = swap(gate_k[1], far_mask)
        og, og_got = onward(og, og_got, far_mask, gate_k[0])
        down_grad = finish([down_k[0], down_got], og[0])
        gate_k, gate_got = onward(gate_k, gate_got, near_mask, down_grad)
        qkv_k, qkv_got = onward(qkv_k, qkv_got, y_mask, gate_k[0])
        og, og_got = onward(og, og_got, near_mask, qkv_k[0])
        lay = down_call(hidden, down_full, og[0])
        lay_f = swap(lay[3], core_mask)
        output_grad = finish([og[0], og_got], lay[0])
        up_k = kept_call(n2_all, dgu, ff, ff, up_got, output_grad)
        up_got = swap(up_k[1], far_mask)
        gate_grad = finish([gate_k[0], gate_got], up_k[0])
        (lay_s,) = sum_call([lay[2], lay_f], [bf16], gate_grad)
        lay_x = swap(lay_s, x_mask)
        qkv_k, qkv_got = onward(qkv_k, qkv_got, far_mask, lay_s)
        lay_c = swap(after(lay[1], qkv_k[0]), core_mask)
        up_k, up_got = onward(up_k, up_got, near_mask, qkv_k[0])
        qkv_k, qkv_got = onward(qkv_k, qkv_got, near_mask, up_k[0])
        (layer_out,) = kernel_call(
            layer_kernel,
            [shape_of(rows, width, bf16)],
            estimate(2 * rows * width * width),
            lay[0],
            lay_c,
            lay_x,
            pick_mlp,
            middle,
            token=qkv_k[0],
        )
        up_grad = finish([up_k[0], up_got], layer_out)
        qkv_grad = finish([qkv_k[0], qkv_got], up_grad)
        q_grad, kv_grad = qkv_grad[:, :qw], qkv_grad[:, qw:]
        down_grad = down_grad.T

        first = jnp.sum(own_attn[:, :wide].astype(f32) * qkv_grad, axis=1)
        first_gain_grad = first / first_gain.astype(f32)
        second = jnp.sum(
            gate_weight.astype(f32) * gate_grad + up_weight.astype(f32) * up_grad, axis=1
        )
        for mask in t_masks:
            second = second + swap(second, mask)
        second = lax.dynamic_slice(second, (t_i * shard,), (shard,))
        second_gain_grad = second / second_gain.astype(f32)

        return (
            layer_out.reshape(tokens.shape),
            input_grad.reshape(tokens.shape),
            first_gain_grad,
            q_grad.reshape(shard, GROUP, KV_HEADS, HEAD).swapaxes(1, 2).reshape(shard, qw),
            kv_grad[:, :kw],
            kv_grad[:, kw:],
            output_grad,
            second_gain_grad,
            gate_grad,
            up_grad,
            down_grad,
        )

    return per_device


def solution(mesh):
    rows = P(None, AXES, None)
    split = P(AXES, None)
    placed = (
        rows,
        rows,
        P(AXES),
        split,
        split,
        split,
        split,
        P(AXES),
        P("dp", "tensor"),
        P("dp", "tensor"),
        P("tensor", "dp"),
        rows,
    )
    return jax.shard_map(
        program(dict(mesh.shape)),
        mesh=mesh,
        in_specs=placed,
        out_specs=(
            rows,
            rows,
            P(AXES),
            split,
            split,
            split,
            split,
            P(AXES),
            P("dp", "tensor"),
            P("dp", "tensor"),
            P("tensor", "dp"),
        ),
        check_vma=False,
    )
```

```python
import functools
import math

import jax
import jax.numpy as jnp
from jax import lax
from jax.experimental import pallas as pl
from jax.experimental.pallas import tpu as pltpu
from jax.sharding import PartitionSpec as P

HEADS = 16
KV_HEADS = 8
HEAD = 96
SLOTS = 6
GROUP = HEADS // KV_HEADS
LANES = 128

EPSILON = 1e-05
ROPE_BASE = 100000.0
NEG_LARGE = -1e30
AXES = ("dp", "tensor")
bf16 = jnp.bfloat16
f32 = jnp.float32


def pack_layout(seq_lengths, row_count):
    seq_ends = jnp.cumsum(seq_lengths)
    seq_starts = seq_ends - seq_lengths
    row_index = jnp.arange(row_count, dtype=jnp.int32)
    segment = jnp.sum((row_index[:, None] >= seq_ends[None, :]).astype(jnp.int32), axis=1)
    owner_hot = segment[:, None] == jnp.arange(seq_lengths.shape[0], dtype=jnp.int32)[None, :]
    position = row_index - jnp.sum(jnp.where(owner_hot, seq_starts[None, :], 0), axis=1)
    return (segment, position)


def rotary_tables(position, head_size):
    half_size = head_size // 2
    freq_index = jnp.arange(half_size, dtype=f32)
    inverse = jnp.exp(freq_index * (-2.0 / head_size) * math.log(ROPE_BASE))
    angles = position.astype(f32)[..., None] * inverse
    return (jnp.cos(angles), jnp.sin(angles))


def product(left_side, right_side):
    return jnp.dot(left_side, right_side, preferred_element_type=f32)


def across(left_side, right_side):
    return lax.dot_general(
        left_side, right_side, (((0,), (0,)), ((), ())), preferred_element_type=f32
    )


def against(left_side, right_side):
    return lax.dot_general(
        left_side, right_side, (((1,), (1,)), ((), ())), preferred_element_type=f32
    )


def bits_of(size):
    return [1 << k for k in range(size.bit_length() - 1)]


def rel_source(me, masks, block, count):
    place = jnp.arange(count, dtype=jnp.int32)
    step = place // block
    delta = jnp.zeros_like(step)
    for k, mask in enumerate(masks):
        delta = delta + ((step >> k) & 1) * mask
    return (me ^ delta) * block + place % block


def join(parts):
    return parts[0] if len(parts) == 1 else jnp.concatenate(parts, axis=0)


BAND = 4 * HEAD


def turn(array, cosine, sine_part):
    lane = lax.broadcasted_iota(jnp.int32, array.shape, 1)
    swapped = jnp.where(
        lane % HEAD < HEAD // 2,
        pltpu.roll(array, BAND - HEAD // 2, 1),
        pltpu.roll(array, HEAD // 2, 1),
    )
    return array * cosine + swapped * sine_part


def head_masks():
    lane = lax.broadcasted_iota(jnp.int32, (1, BAND), 1)
    return [jnp.where(lane // HEAD == h, 1.0, 0.0) for h in range(4)]


def stack_heads(bands, masks):
    return jnp.concatenate([band * mask.astype(bf16) for band in bands for mask in masks], axis=0)


def unstack_heads(stacked, masks, per_pack):
    found = []
    for g in range(GROUP):
        total = 0.0
        for h in range(4):
            first = (g * 4 + h) * per_pack
            total = total + stacked[first : first + per_pack] * masks[h]
        found.append(total)
    return found


def pack_probs(stacked, keys, allowed):
    per_pack = keys.shape[0]
    scores = against(stacked, keys) * (1.0 / math.sqrt(HEAD))
    scores = scores.reshape(-1, per_pack, per_pack)
    peak = jnp.max(jnp.where(allowed, scores, NEG_LARGE), axis=-1, keepdims=True)
    raised = jnp.where(allowed, jnp.exp(jnp.where(allowed, scores - peak, 0.0)), 0.0)
    totals = jnp.sum(raised, axis=-1, keepdims=True)
    return raised / jnp.where(totals > 0, totals, 1.0)


def columns(band):
    return pl.ds(band * BAND, BAND)


def piece_rows(pieces, place, mixed):
    if not mixed:
        return jnp.concatenate([piece[:, place] for piece in pieces], axis=0)
    n = pieces[0].shape[0] // 2
    found = []
    for a, b in (pieces[:2], pieces[2:]):
        for k in (slice(0, n), slice(n, 2 * n)):
            found += [a[k, place], b[k, place]]
    return jnp.concatenate(found, axis=0)


def forward_kernel(micro, per_pack, kv_bands, *refs):
    x_ref, cos_ref, sin_ref, mask_ref, *piece_refs = refs[:-4]
    qkv_ref, att_ref, n1_ref, gains_ref = refs[-4:]
    q_bands = GROUP * kv_bands
    q_refs, kv_refs = piece_refs[:4], piece_refs[4:]
    skip = q_bands // 2
    tail = pl.ds((skip + 2 * kv_bands) * BAND, LANES)
    gains = jnp.transpose(piece_rows(kv_refs, tail, False).astype(f32))
    gains_ref[...] = gains[: gains_ref.shape[0]]
    inputs = x_ref[...].astype(f32)
    scale = lax.rsqrt(jnp.mean(inputs * inputs, axis=1, keepdims=True) + EPSILON)
    n1_ref[...] = (inputs * scale * gains[:1]).astype(bf16)
    for band in range(q_bands + 2 * kv_bands):
        in_q = band < q_bands
        place = columns(band if in_q else band - q_bands + skip)
        total = product(n1_ref[...], piece_rows(q_refs if in_q else kv_refs, place, in_q))
        if band < q_bands + kv_bands:
            total = turn(total, cos_ref[...], sin_ref[...])
        qkv_ref[:, columns(band)] = total.astype(bf16)

    masks = head_masks()

    def one_pack(pack, carry):
        rows = pl.ds(pl.multiple_of(pack * per_pack, per_pack), per_pack)
        allowed = (mask_ref[pl.ds(pack, 1)] > 0.0)
        for j in range(kv_bands):
            bands = [g * kv_bands + j for g in range(GROUP)]
            stacked = stack_heads([qkv_ref[rows, columns(b)] for b in bands], masks)
            keys = qkv_ref[rows, columns(q_bands + j)]
            values = qkv_ref[rows, columns(q_bands + kv_bands + j)]
            probs = pack_probs(stacked, keys, allowed)
            mixed = product(probs.astype(bf16).reshape(-1, per_pack), values)
            for b, band in zip(bands, unstack_heads(mixed, masks, per_pack)):
                att_ref[rows, columns(b)] = band.astype(bf16)
        return carry

    lax.fori_loop(0, micro, one_pack, 0)


def pack_kernel(q_ref, k_ref, v_ref, gains_ref, o_ref, out_ref):
    heads = [
        q_ref[:, (k * GROUP + g) * HEAD : (k * GROUP + g + 1) * HEAD]
        for g in range(GROUP)
        for k in range(KV_HEADS)
    ]
    first = 0
    for piece in (
        jnp.concatenate(heads, axis=1), o_ref[...], k_ref[...], v_ref[...], gains_ref[...]
    ):
        out_ref[:, first : first + piece.shape[1]] = piece
        first += piece.shape[1]


def backward_kernel(micro, per_pack, kv_bands, *refs):
    dmb_ref, qkv_ref, cos_ref, sin_ref, mask_ref, pick_ref, *piece_refs = refs[:14]
    dqkv_ref, datt_ref = refs[-2:]
    half = pick_ref.shape[1] // 2
    everything = slice(None)
    datt = against(dmb_ref[:, :half], piece_rows(piece_refs[:4], everything, True))
    datt = datt + against(dmb_ref[:, half:], piece_rows(piece_refs[4:], everything, False))
    datt_ref[...] = against(datt.astype(bf16), pick_ref[...]).astype(bf16)
    q_bands = GROUP * kv_bands
    factor = 1.0 / math.sqrt(HEAD)
    masks = head_masks()

    def one_pack(pack, carry):
        rows = pl.ds(pl.multiple_of(pack * per_pack, per_pack), per_pack)
        allowed = (mask_ref[pl.ds(pack, 1)] > 0.0)
        cosine, sine_part = cos_ref[rows, :], -sin_ref[rows, :]
        for j in range(kv_bands):
            bands = [g * kv_bands + j for g in range(GROUP)]
            stacked = stack_heads([qkv_ref[rows, columns(b)] for b in bands], masks)
            keys = qkv_ref[rows, columns(q_bands + j)]
            values = qkv_ref[rows, columns(q_bands + kv_bands + j)]
            grads = stack_heads([datt_ref[rows, columns(b)] for b in bands], masks)
            probs = pack_probs(stacked, keys, allowed)
            dprob = against(grads, values).reshape(probs.shape)
            delta = jnp.sum(probs * dprob, axis=-1, keepdims=True)
            dscore = (probs * (dprob - delta)).astype(bf16).reshape(-1, per_pack)
            dvalue = across(probs.astype(bf16).reshape(-1, per_pack), grads)
            dkey = turn(across(dscore, stacked) * factor, cosine, sine_part)
            dquery = product(dscore, keys) * factor
            for b, band in zip(bands, unstack_heads(dquery, masks, per_pack)):
                dqkv_ref[rows, columns(b)] = turn(band, cosine, sine_part).astype(bf16)
            dqkv_ref[rows, columns(q_bands + j)] = dkey.astype(bf16)
            dqkv_ref[rows, columns(q_bands + kv_bands + j)] = dvalue.astype(bf16)
        return carry

    lax.fori_loop(0, micro, one_pack, 0)


def mlp_kernel(ff, *refs):
    weight_refs = refs[4:8]
    gu_refs, down_refs = weight_refs[:2], weight_refs[2:]
    first = pl.program_id(0) == 0
    n2_ref = jnp.where(first, refs[0][...], refs[1][...])
    dy_ref = jnp.where(first, refs[2][...], refs[3][...])
    hidden_ref, dgu_ref, *dn2_refs = refs[-4:]
    half = gu_refs[0].shape[0]
    lower, upper = slice(0, half), slice(half, 2 * half)
    both = product(n2_ref[:, lower], gu_refs[0][...]) + product(n2_ref[:, upper], gu_refs[1][...])
    gate, up = both[:, :ff], both[:, ff:]
    dhid = product(dy_ref[:, lower], down_refs[0][...])
    dhid = dhid + product(dy_ref[:, upper], down_refs[1][...])
    sig = jax.nn.sigmoid(gate)
    passed = gate * sig
    hidden_ref[...] = (passed * up).astype(bf16)
    dgu_ref[:, :ff] = (dhid * up * sig * (1.0 + gate * (1.0 - sig))).astype(bf16)
    dgu_ref[:, ff:] = (dhid * passed).astype(bf16)
    dgu = dgu_ref[...]
    dn2 = jnp.concatenate([against(dgu, gu[...]).astype(bf16) for gu in gu_refs], axis=1)
    put_by_step(dn2_refs, [dn2] * 2)


def put_by_step(refs, values):
    for k, (ref, value) in enumerate(zip(refs, values)):

        @pl.when(pl.program_id(0) == k)
        def _(ref=ref, value=value):
            ref[...] = value.astype(ref.dtype)


def shape_of(rows, columns, kind):
    return jax.ShapeDtypeStruct((rows, columns), kind)


def estimate(flops):
    return pl.CostEstimate(flops=100000000000, bytes_accessed=0, transcendentals=0)


SHORT = pl.CostEstimate(flops=10**9, bytes_accessed=0, transcendentals=0)
LIMIT = pltpu.CompilerParams(vmem_limit_bytes=56 * 1024 * 1024)
ANYWHERE = pl.BlockSpec(memory_space=pl.ANY)


def fixed(rows, columns, row=0, column=0):
    return pl.BlockSpec((rows, columns), lambda i: (row, column))


def mlp_call(first, n2, dy, weights, *earlier):
    block, width = n2[0][0].shape[0], n2[0][0].shape[1]
    rows = 4 * block
    ff = weights[-1].shape[1]

    def band(columns):
        return pl.BlockSpec((block, columns), lambda i: (first + 2 * i, 0))

    return pl.pallas_call(
        functools.partial(mlp_kernel, ff),
        grid=(2,),
        in_specs=[fixed(block, width, row) for _, row in n2 + dy]
        + [fixed(*array.shape) for array in weights]
        + [ANYWHERE] * len(earlier),
        out_specs=[band(ff), band(2 * ff), fixed(block, width), fixed(block, width)],
        out_shape=[shape_of(rows, ff, bf16), shape_of(rows, 2 * ff, bf16)]
        + [shape_of(block, width, bf16)] * 2,
        input_output_aliases={8 + k: k for k in range(len(earlier) - 1)},
        compiler_params=LIMIT,
        cost_estimate=estimate(10 * 2 * block * width * ff),
    )(*[array for array, _ in n2 + dy], *weights, *earlier)


def left_rows(refs):
    return refs[0][...] if len(refs) == 1 else jnp.concatenate([r[...] for r in refs], axis=0)


def left_parts(left, right):
    if not isinstance(left, list):
        left = [(left, 0)]
    return left, right.shape[0] // len(left), left[0][0].shape[1]


def sent_kernel(*refs):
    right_ref, _, out_ref = refs[-3:]
    out_ref[...] = across(left_rows(refs[:-3]), right_ref[...]).astype(bf16)


def sent_call(left, right, at, columns, token):
    left, count, width = left_parts(left, right)
    block = width // 4
    return pl.pallas_call(
        sent_kernel,
        grid=(2,),
        in_specs=[
            pl.BlockSpec((count, block), lambda i, row=row: (row, 2 + i)) for _, row in left
        ]
        + [fixed(right.shape[0], columns, 0, at // columns), ANYWHERE],
        out_specs=pl.BlockSpec((block, columns), lambda i: (i, 0)),
        out_shape=shape_of(2 * block, columns, bf16),
        compiler_params=LIMIT,
        cost_estimate=estimate(4 * count * block * columns),
    )(*[array for array, _ in left], right, token)


def kept_kernel(*refs):
    right_ref, got_ref, _, keep_ref, send_ref = refs[-5:]
    total = across(left_rows(refs[:-5]), right_ref[...]) + got_ref[...].astype(f32)
    put_by_step((keep_ref, send_ref), (total, total))


def kept_call(left, right, at, columns, got, token):
    left, count, width = left_parts(left, right)
    block = width // 4
    return pl.pallas_call(
        kept_kernel,
        grid=(2,),
        in_specs=[pl.BlockSpec((count, block), lambda i, row=row: (row, i)) for _, row in left]
        + [
            fixed(right.shape[0], columns, 0, at // columns),
            pl.BlockSpec((block, columns), lambda i: (i, 0)),
            ANYWHERE,
        ],
        out_specs=[fixed(block, columns)] * 2,
        out_shape=[shape_of(block, columns, f32), shape_of(block, columns, bf16)],
        compiler_params=LIMIT,
        cost_estimate=estimate(4 * count * block * columns),
    )(*[array for array, _ in left], right, got, token)


def sum_kernel(count, *refs):
    total = 0.0
    for ref in refs[:count]:
        total = total + ref[...].astype(f32)
    outs = refs[count + 1 :]
    rows = total.shape[0] // len(outs)
    for k, out in enumerate(outs):
        out[...] = total[k * rows : (k + 1) * rows].astype(out.dtype)


def sum_call(arrays, kinds, token):
    rows, columns = arrays[0].shape
    block = columns // 2 if columns % 256 == 0 else columns
    part = rows // len(kinds)
    return pl.pallas_call(
        functools.partial(sum_kernel, len(arrays)),
        grid=(columns // block,),
        in_specs=[pl.BlockSpec((rows, block), lambda i: (0, i))] * len(arrays) + [ANYWHERE],
        out_specs=[pl.BlockSpec((part, block), lambda i: (0, i))] * len(kinds),
        out_shape=[shape_of(part, columns, kind) for kind in kinds],
        compiler_params=LIMIT,
        cost_estimate=estimate(rows * columns),
    )(*arrays, token)


def norm_back(upstream, signal, gain):
    inverse = lax.rsqrt(jnp.mean(signal * signal, axis=1, keepdims=True) + EPSILON)
    weighted = upstream * gain
    mixed = jnp.mean(weighted * signal, axis=1, keepdims=True)
    return inverse * weighted - signal * (inverse * inverse * inverse) * mixed


def second_norm_kernel(*refs):
    near_ref, core_ref, x_ref, pick_ref, dy_ref, middle_ref, gain_ref, _ = refs[:8]
    dmid_ref, dmb_ref = refs[8:]
    dn2 = near_ref[...].astype(f32) + core_ref[...].astype(f32) + x_ref[...].astype(f32)
    dn2 = against(dn2.astype(bf16), pick_ref[...])
    dmid = dy_ref[...].astype(f32) + norm_back(dn2, middle_ref[...], gain_ref[...])
    dmid_ref[...] = dmid
    dmb_ref[...] = dmid.astype(bf16)


def first_norm_kernel(band, *refs):
    dqkv_ref, x_ref, gains_ref, pick_ref, dmid_ref, *piece_refs = refs[:-2]
    out_ref = refs[-1]
    dn1 = 0.0
    bands = dqkv_ref.shape[1] // band
    for k in range(bands):
        in_q = k < bands // 2
        place = pl.ds((k if in_q else k - bands // 2 + 1) * band, band)
        found = piece_rows(piece_refs[:4] if in_q else piece_refs[4:], place, in_q)
        dn1 = dn1 + against(dqkv_ref[:, pl.ds(k * band, band)], found)
    part = norm_back(dn1, x_ref[...].astype(f32), gains_ref[:1])
    high = part.astype(bf16)
    low = (part - high.astype(f32)).astype(bf16)
    out_ref[...] = dmid_ref[...] + against(high, pick_ref[...]) + against(low, pick_ref[...])


def down_kernel(hidden_ref, near_ref, far_ref, token_ref, *out_refs):
    parts = [against(hidden_ref[...], ref[...]) for ref in (near_ref, far_ref)]
    rows = jnp.concatenate(parts, axis=1)
    put_by_step(out_refs, [rows] * 4)


def down_call(hidden, near, far, token):
    rows, ff = hidden.shape
    width, block = 2 * near.shape[0], hidden.shape[0] // 4
    return pl.pallas_call(
        down_kernel,
        grid=(4,),
        in_specs=[pl.BlockSpec((block, ff), lambda i: (i, 0))]
        + [fixed(*near.shape), fixed(*far.shape), ANYWHERE],
        out_specs=[fixed(block, width)] * 4,
        out_shape=[shape_of(block, width, bf16)] * 4,
        compiler_params=LIMIT,
        cost_estimate=estimate(2 * rows * width * ff),
    )(hidden, near, far, token)


def layer_kernel(own_ref, core_ref, x_ref, pick_ref, middle_ref, token_ref, out_ref):
    total = own_ref[...].astype(f32) + core_ref[...].astype(f32) + x_ref[...].astype(f32)
    total = middle_ref[...] + against(total.astype(bf16), pick_ref[...])
    out_ref[...] = total.astype(bf16)


def join_kernel(plan, *refs):
    outs = refs[-len(plan) :]
    for out, pieces in zip(outs, plan):
        first, width = 0, out.shape[1]
        for k, column in pieces:
            rows = refs[k].shape[0]
            out[first : first + rows, :] = refs[k][:, column : column + width]
            first += rows


def pick_kernel(*refs):
    for source, out in zip(refs[:3], refs[-3:]):
        rows = lax.broadcasted_iota(jnp.int32, out.shape, 0)
        out[...] = jnp.where(rows == source[...], 1.0, 0.0).astype(bf16)


def order_kernel(count, *refs):
    pick_ref, out_ref = refs[count], refs[-1]
    n = refs[0].shape[0]
    for k, ref in enumerate(refs[:count]):
        out_ref[k * n : (k + 1) * n, :] = product(ref[...], pick_ref[...]).astype(bf16)


def two_kernel(*refs):
    gu_z, down_z, xs_y, ys_x = refs[:4]
    both_ref, xs_ref, ys_ref = refs[-3:]
    columns = gu_z.shape[1]
    both_ref[:, :columns], both_ref[:, columns:] = gu_z[...], down_z[...]
    xs_ref[...] = xs_y[...]
    ys_ref[...] = ys_x[...]


def join_call(arrays, plan, widths, token):
    outs = [
        shape_of(sum(arrays[k].shape[0] for k, _ in pieces), width, bf16)
        for pieces, width in zip(plan, widths)
    ]
    return kernel_call(
        functools.partial(join_kernel, plan), outs, estimate(0), *arrays, token=token
    )


def output_kernel(*refs):
    att_ref, pick_out_ref, x_ref, gain_ref, pick_mlp_ref, *piece_refs = refs[:13]
    rel_ref, middle_ref, n2_ref = refs[-3:]
    att = product(att_ref[...], pick_out_ref[...]).astype(bf16)
    rel_ref[...] = att
    everything = slice(None)
    left = product(att, piece_rows(piece_refs[:4], everything, True))
    right = product(att, piece_rows(piece_refs[4:], everything, False))
    middle = x_ref[...].astype(f32) + jnp.concatenate([left, right], axis=1)
    middle_ref[...] = middle
    scale = lax.rsqrt(jnp.mean(middle * middle, axis=1, keepdims=True) + EPSILON)
    n2 = (middle * scale * gain_ref[...]).astype(bf16)
    n2_ref[...] = product(n2, pick_mlp_ref[...]).astype(bf16)


def kernel_call(body, outs, cost, *args, token=(), scratch=()):
    tokens = token if isinstance(token, tuple) else (token,)
    arrays, specs = [], []

    def alone(shape, place=None):
        where = (0,) * len(shape) if place is None else (0, place)
        return pl.BlockSpec(shape, lambda i: where, pipeline_mode=pl.Buffered(1))

    for arg in args:
        array, (columns, place) = arg if isinstance(arg, tuple) else (arg, (None, None))
        arrays.append(array)
        shape = array.shape if columns is None else (array.shape[0], columns)
        specs.append(alone(shape, place))
    return pl.pallas_call(
        body,
        grid=(1,),
        out_shape=outs,
        in_specs=specs + [ANYWHERE] * len(tokens),
        out_specs=[alone(out.shape) for out in outs],
        scratch_shapes=list(scratch),
        compiler_params=LIMIT,
        cost_estimate=cost,
    )(*arrays, *tokens)


def after(array, *others):
    return lax.optimization_barrier((array,) + others)[0]


def together(*arrays):
    return lax.optimization_barrier(arrays)


def program(sizes):
    dp_n, tp_n = sizes["dp"], sizes["tensor"]
    world = dp_n * tp_n

    def swap(array, mask):
        return lax.ppermute(array, AXES, [(i, i ^ mask) for i in range(world)])

    dp_bits = [m * tp_n for m in bits_of(dp_n)]
    y_mask, z_masks = dp_bits[0], dp_bits[:0:-1]
    t_masks = bits_of(tp_n)[::-1]
    x_mask, core_mask = t_masks
    attn_masks = z_masks + [y_mask, x_mask, core_mask]
    mlp_masks = z_masks + [y_mask]

    def gather_far(own):
        if len(z_masks) == 2:
            one, two = z_masks
            return [own, swap(own, one), swap(own, two), swap(own, one ^ two)]
        held = own
        for mask in z_masks:
            held = join([held, swap(held, mask)])
        return [held]

    def finish(pair, token):
        (total,) = sum_call(pair, [f32], token)
        for mask in z_masks[:-2][::-1]:
            n = total.shape[0] // 2
            total = total[:n] + swap(total[n:].astype(bf16), mask).astype(f32)
        return total

    def per_device(
        tokens,
        lengths,
        first_gain,
        query_weight,
        key_weight,
        value_weight,
        output_weight,
        second_gain,
        gate_weight,
        up_weight,
        down_weight,
        cotangent,
    ):
        micro, per_pack, width = tokens.shape
        rows = micro * per_pack
        qw, kw = query_weight.shape[1], key_weight.shape[1]
        ff = gate_weight.shape[1]
        wide = qw + 2 * kw
        shard = query_weight.shape[0]
        dp_i, t_i = lax.axis_index("dp"), lax.axis_index("tensor")
        me = dp_i * tp_n + t_i

        x_low = tokens.reshape(rows, width)
        dy_low = cotangent.reshape(rows, width)
        half, quarter = width // 2, width // 4

        gains = jnp.pad(
            jnp.stack([first_gain, second_gain], axis=1), ((0, 0), (0, LANES - 2))
        )
        (own_attn,) = kernel_call(
            pack_kernel,
            [jax.ShapeDtypeStruct((shard, 2 * qw + 2 * kw + LANES), bf16)],
            None,
            query_weight,
            key_weight,
            value_weight,
            gains,
            output_weight,
        )
        own_gu = jnp.concatenate([gate_weight, up_weight], axis=1)
        own_down = down_weight.T
        own_mlp = jnp.concatenate([own_gu, own_down], axis=1)

        attn_source = rel_source(me, attn_masks, shard, width)
        head, lane = attn_source // HEAD, attn_source % HEAD
        out_source = (head % GROUP * KV_HEADS + head // GROUP) * HEAD + lane
        mlp_source = rel_source(dp_i, [m // tp_n for m in mlp_masks], shard * tp_n, width)

        def restore(array, pick):
            return against(array, pick)

        far = gather_far(own_attn)
        mlp_y = swap(own_mlp, y_mask)
        dy_x = swap(dy_low, x_mask)
        widths = (qw + half, half + 2 * kw + LANES)
        at = (0, widths[0])
        xs_four, ys_four = join_call(
            far, [[(k, first) for k in range(len(far))] for first in at], widths, (dy_x, mlp_y)
        )

        xs_x = swap(xs_four, x_mask)
        ys_y = swap(ys_four, y_mask)
        down_z = swap(after(own_down, xs_four), z_masks[0])
        pairs = (xs_four, xs_x, ys_four, ys_y)
        xs_eight, ys_eight = join_call(
            pairs, [[(2 * k, 0), (2 * k + 1, 0)] for k in range(2)], widths, down_z
        )

        xs_y = swap(xs_eight, y_mask)
        ys_x = swap(ys_eight, x_mask)
        gu_z = swap(after(own_gu, xs_eight), z_masks[0])
        mlp_far = swap(after(own_mlp, xs_eight), z_masks[1])
        xs_c = swap(xs_eight, core_mask)
        mlp_z, xs_far, ys_far = kernel_call(
            two_kernel,
            [
                shape_of(*own_mlp.shape, bf16),
                shape_of(*xs_y.shape, bf16),
                shape_of(*ys_x.shape, bf16),
            ],
            SHORT,
            gu_z,
            down_z,
            xs_y,
            ys_x,
            token=(xs_c, mlp_far),
        )
        ys_c = swap(after(ys_eight, mlp_z), core_mask)
        pick_attn, pick_out, pick_mlp = kernel_call(
            pick_kernel,
            [shape_of(width, width, bf16)] * 3,
            SHORT,
            *[source[None, :] for source in (attn_source, out_source, mlp_source)],
            token=mlp_z,
        )
        (x_rel,) = kernel_call(
            functools.partial(order_kernel, 1),
            [shape_of(rows, width, bf16)],
            SHORT,
            x_low,
            pick_attn,
        )

        x_pieces = [xs_eight, xs_y, xs_c, swap(xs_far, core_mask)]
        y_pieces = [ys_eight, ys_x, ys_c, swap(ys_far, core_mask)]
        q_pieces = [(piece, (qw, 0)) for piece in x_pieces]
        left_pieces = [(piece, (half, qw // half)) for piece in x_pieces]
        right_pieces = [(piece, (half, 0)) for piece in y_pieces]
        mlp_y1 = swap(mlp_z, y_mask)
        mlp_near = swap(mlp_z, z_masks[1])

        segment, position = jax.vmap(lambda own: pack_layout(own, per_pack))(lengths[:, 0])
        cosine, sine_part = rotary_tables(position, HEAD)
        row_index = jnp.arange(per_pack, dtype=jnp.int32)
        allowed = (
            (segment[:, :, None] == segment[:, None, :])
            & (row_index[None, None, :] <= row_index[None, :, None])
            & (segment < SLOTS - 1)[:, :, None]
        ).astype(f32)

        half_tables = (cosine.reshape(rows, -1), sine_part.reshape(rows, -1))
        cos_band = jnp.tile(half_tables[0], (1, BAND // half_tables[0].shape[1]))
        sin_band = jnp.tile(jnp.concatenate([-half_tables[1], half_tables[1]], axis=1), (1, 4))
        kv_bands = kw // BAND
        shapes = (micro, per_pack, kv_bands)
        cost = pl.CostEstimate(
            flops=100000000000, bytes_accessed=0, transcendentals=0
        )
        qkv, attended, n1_rel, gains_rel = kernel_call(
            functools.partial(forward_kernel, *shapes),
            [
                jax.ShapeDtypeStruct((rows, wide), bf16),
                jax.ShapeDtypeStruct((rows, qw), bf16),
                jax.ShapeDtypeStruct((rows, width), bf16),
                jax.ShapeDtypeStruct((8, width), f32),
            ],
            cost,
            x_rel,
            cos_band,
            sin_band,
            allowed,
            *q_pieces,
            *y_pieces,
        )
        g2 = restore(gains_rel[1:2].astype(bf16), pick_attn)
        (mlp_last,) = join_call(
            (mlp_far, mlp_near), [[(0, 0), (1, 0)]], [3 * ff], (attended, mlp_y1)
        )
        mlp_y2 = swap(mlp_last, y_mask)
        att_rel, middle, n2_rel = kernel_call(
            output_kernel,
            [shape_of(rows, qw, bf16), shape_of(rows, width, f32), shape_of(rows, width, bf16)],
            estimate(6 * rows * width * width),
            attended,
            pick_out,
            x_low,
            g2,
            pick_mlp,
            *left_pieces,
            *right_pieces,
            token=mlp_last,
        )

        n2_x = swap(n2_rel, x_mask)
        n2_c = swap(n2_rel, core_mask)
        (dy_near,) = kernel_call(
            functools.partial(order_kernel, 2),
            [shape_of(2 * rows, width, bf16)],
            estimate(0),
            dy_low,
            dy_x,
            pick_mlp,
            token=n2_rel,
        )
        dy_c = swap(dy_near, core_mask)
        near_parts, far_parts = (own_mlp, mlp_z, mlp_last), (mlp_y, mlp_y1, mlp_y2)
        for mask in z_masks[2:]:
            near_parts = near_parts + (swap(join(near_parts), mask),)
            far_parts = far_parts + (swap(near_parts[-1], y_mask),)

        def assemble(parts, token):
            plan = [[(k, 0) for k in range(len(parts))], [(k, 2 * ff) for k in range(len(parts))]]
            return join_call(parts, plan, (2 * ff, ff), token)

        gu_near, down_near = assemble(near_parts, dy_near)
        (n2_f,) = join_call((n2_x,), [[(0, 0)]], [width], (far_parts[-1], gu_near))
        n2_xc = swap(n2_f, core_mask)
        gu_far, down_far = assemble(far_parts, n2_f)
        weights = (gu_near, gu_far, down_near, down_far)
        n2_all = [(n2_rel, 0), (n2_x, 0), (n2_c, 0), (n2_xc, 0)]
        dy_all = [(dy_near, 0), (dy_near, 1), (dy_c, 0), (dy_c, 1)]
        weights = (gu_near, gu_far, down_near, down_far)
        *grown, far_own, far_send = mlp_call(
            1, n2_all[1::2], dy_all[1::2], weights, gu_far
        )
        far_c = swap(far_send, core_mask)
        (dn2_sum,) = sum_call([far_own, far_c], [bf16], far_own)
        dn2_x = swap(dn2_sum, x_mask)
        hidden, dgu, near_own, near_send = mlp_call(
            0, n2_all[::2], dy_all[::2], weights, *grown, dn2_sum
        )
        near_c = swap(near_send, core_mask)
        down_b = sent_call(dy_all, hidden, 0, ff, near_own)
        down_got = swap(down_b, y_mask)

        dmid, dmb = kernel_call(
            second_norm_kernel,
            [shape_of(rows, width, f32), shape_of(rows, width, bf16)],
            estimate(4 * rows * width * width),
            near_own,
            near_c,
            dn2_x,
            pick_mlp,
            dy_low,
            middle,
            g2,
            token=down_b,
        )
        (dqkv,) = kernel_call(
            functools.partial(backward_kernel, *shapes),
            [shape_of(rows, wide, bf16)],
            cost,
            dmb,
            qkv,
            cos_band,
            sin_band,
            allowed,
            pick_out,
            *left_pieces,
            *right_pieces,
            scratch=[pltpu.VMEM((rows, qw), bf16)],
        )
        qkv_b = sent_call(n1_rel, dqkv, 0, wide, dqkv)
        qkv_c = swap(qkv_b, core_mask)
        gate_b = sent_call(n2_all, dgu, 0, ff, qkv_b)
        gate_got = swap(gate_b, y_mask)
        far_mask, near_mask = z_masks[-1], z_masks[-2]
        step = [f32, bf16]

        def onward(pair, got, mask, token):
            pair = sum_call([pair[0], got], step, token)
            return pair, swap(pair[1], mask)

        qkv_k = kept_call(n1_rel, dqkv, 0, wide, qkv_c, gate_b)
        qkv_got = swap(qkv_k[1], x_mask)
        down_k = kept_call(dy_all, hidden, 0, ff, down_got, qkv_k[0])
        down_got = swap(down_k[1], far_mask)
        up_b = sent_call(n2_all, dgu, ff, ff, down_k[0])
        up_got = swap(up_b, y_mask)
        gate_k = kept_call(n2_all, dgu, 0, ff, gate_got, up_b)
        gate_got = swap(gate_k[1], far_mask)
        (input_grad,) = kernel_call(
            functools.partial(first_norm_kernel, 2 * BAND),
            [shape_of(rows, width, f32)],
            estimate(2 * rows * width * (wide + 2 * width)),
            dqkv,
            x_rel,
            gains_rel,
            pick_attn,
            dmid,
            *q_pieces,
            *y_pieces,
            token=gate_k[0],
        )
        down_k, down_got = onward(down_k, down_got, near_mask, input_grad)
        gate_k, gate_got = onward(gate_k, gate_got, near_mask, down_k[0])
        up_k = kept_call(n2_all, dgu, ff, ff, up_got, gate_k[0])
        up_got = swap(up_k[1], far_mask)
        og_b = sent_call(att_rel, dmb, 0, width, up_k[0])
        og_c = swap(og_b, core_mask)
        down_grad = finish([down_k[0], down_got], og_b)
        qkv_k, qkv_got = onward(qkv_k, qkv_got, y_mask, down_grad)
        og = kept_call(att_rel, dmb, 0, width, og_c, qkv_k[0])
        og_got = swap(og[1], x_mask)
        gate_grad = finish([gate_k[0], gate_got], og[0])
        up_k, up_got = onward(up_k, up_got, near_mask, gate_grad)
        lay = down_call(hidden, *weights[2:], up_k[0])
        lay_f = swap(lay[3], core_mask)
        og, og_got = onward(og, og_got, y_mask, lay[0])
        (lay_s,) = sum_call([lay[1], lay_f], [bf16], og[0])
        lay_x = swap(lay_s, x_mask)
        qkv_k, qkv_got = onward(qkv_k, qkv_got, far_mask, lay_s)
        og, og_got = onward(og, og_got, far_mask, qkv_k[0])
        lay_c = swap(after(lay[2], og[0]), core_mask)
        up_grad = finish([up_k[0], up_got], og[0])
        qkv_k, qkv_got = onward(qkv_k, qkv_got, near_mask, up_grad)
        og, og_got = onward(og, og_got, near_mask, qkv_k[0])
        (layer_out,) = kernel_call(
            layer_kernel,
            [shape_of(rows, width, bf16)],
            estimate(2 * rows * width * width),
            lay[0],
            lay_c,
            lay_x,
            pick_mlp,
            middle,
            token=og[0],
        )
        qkv_grad = finish([qkv_k[0], qkv_got], layer_out)
        output_grad = finish([og[0], og_got], qkv_grad)
        q_grad, kv_grad = qkv_grad[:, :qw], qkv_grad[:, qw:]
        down_grad = down_grad.T

        first = jnp.sum(own_attn[:, :qw].astype(f32) * q_grad, axis=1)
        own_kv = own_attn[:, qw + width : qw + width + 2 * kw].astype(f32)
        first = first + jnp.sum(own_kv * kv_grad, axis=1)
        first_gain_grad = first / first_gain.astype(f32)
        second = jnp.sum(
            gate_weight.astype(f32) * gate_grad + up_weight.astype(f32) * up_grad, axis=1
        )
        for mask in t_masks:
            second = second + swap(second, mask)
        second = lax.dynamic_slice(second, (t_i * shard,), (shard,))
        second_gain_grad = second / second_gain.astype(f32)

        return (
            layer_out.reshape(tokens.shape),
            input_grad.reshape(tokens.shape),
            first_gain_grad,
            q_grad.reshape(shard, GROUP, KV_HEADS, HEAD).swapaxes(1, 2).reshape(shard, qw),
            kv_grad[:, :kw],
            kv_grad[:, kw:],
            output_grad,
            second_gain_grad,
            gate_grad,
            up_grad,
            down_grad,
        )

    return per_device


def solution(mesh):
    rows = P(None, AXES, None)
    split = P(AXES, None)
    placed = (
        rows,
        rows,
        P(AXES),
        split,
        split,
        split,
        split,
        P(AXES),
        P("dp", "tensor"),
        P("dp", "tensor"),
        P("tensor", "dp"),
        rows,
    )
    return jax.shard_map(
        program(dict(mesh.shape)),
        mesh=mesh,
        in_specs=placed,
        out_specs=(
            rows,
            rows,
            P(AXES),
            split,
            split,
            split,
            split,
            P(AXES),
            P("dp", "tensor"),
            P("dp", "tensor"),
            P("tensor", "dp"),
        ),
        check_vma=False,
    )
```

```python
import functools
import math

import jax
import jax.numpy as jnp
from jax import lax
from jax.experimental import pallas as pl
from jax.experimental.pallas import tpu as pltpu
from jax.sharding import PartitionSpec as P

HEADS = 16
KV_HEADS = 8
HEAD = 96
SLOTS = 6
GROUP = HEADS // KV_HEADS
LANES = 128

EPSILON = 1e-05
ROPE_BASE = 100000.0
NEG_LARGE = -1e30
AXES = ("dp", "tensor")
bf16 = jnp.bfloat16
f32 = jnp.float32


def pack_layout(seq_lengths, row_count):
    seq_ends = jnp.cumsum(seq_lengths)
    seq_starts = seq_ends - seq_lengths
    row_index = jnp.arange(row_count, dtype=jnp.int32)
    segment = jnp.sum((row_index[:, None] >= seq_ends[None, :]).astype(jnp.int32), axis=1)
    owner_hot = segment[:, None] == jnp.arange(seq_lengths.shape[0], dtype=jnp.int32)[None, :]
    position = row_index - jnp.sum(jnp.where(owner_hot, seq_starts[None, :], 0), axis=1)
    return (segment, position)


def rotary_tables(position, head_size):
    half_size = head_size // 2
    freq_index = jnp.arange(half_size, dtype=f32)
    inverse = jnp.exp(freq_index * (-2.0 / head_size) * math.log(ROPE_BASE))
    angles = position.astype(f32)[..., None] * inverse
    return (jnp.cos(angles), jnp.sin(angles))


def product(left_side, right_side):
    return jnp.dot(left_side, right_side, preferred_element_type=f32)


def across(left_side, right_side):
    return lax.dot_general(
        left_side, right_side, (((0,), (0,)), ((), ())), preferred_element_type=f32
    )


def against(left_side, right_side):
    return lax.dot_general(
        left_side, right_side, (((1,), (1,)), ((), ())), preferred_element_type=f32
    )


def bits_of(size):
    return [1 << k for k in range(size.bit_length() - 1)]


def rel_source(me, masks, block, count):
    place = jnp.arange(count, dtype=jnp.int32)
    step = place // block
    delta = jnp.zeros_like(step)
    for k, mask in enumerate(masks):
        delta = delta + ((step >> k) & 1) * mask
    return (me ^ delta) * block + place % block


def join(parts):
    return parts[0] if len(parts) == 1 else jnp.concatenate(parts, axis=0)


BAND = 4 * HEAD


def turn(array, cosine, sine_part):
    lane = lax.broadcasted_iota(jnp.int32, array.shape, 1)
    swapped = jnp.where(
        lane % HEAD < HEAD // 2,
        pltpu.roll(array, BAND - HEAD // 2, 1),
        pltpu.roll(array, HEAD // 2, 1),
    )
    return array * cosine + swapped * sine_part


def head_masks():
    lane = lax.broadcasted_iota(jnp.int32, (1, BAND), 1)
    return [jnp.where(lane // HEAD == h, 1.0, 0.0) for h in range(4)]


def stack_heads(bands, masks):
    return jnp.concatenate([band * mask.astype(bf16) for band in bands for mask in masks], axis=0)


def unstack_heads(stacked, masks, per_pack):
    found = []
    for g in range(GROUP):
        total = 0.0
        for h in range(4):
            first = (g * 4 + h) * per_pack
            total = total + stacked[first : first + per_pack] * masks[h]
        found.append(total)
    return found


def pack_probs(stacked, keys, allowed):
    per_pack = keys.shape[0]
    scores = against(stacked, keys) * (1.0 / math.sqrt(HEAD))
    scores = scores.reshape(-1, per_pack, per_pack)
    peak = jnp.max(jnp.where(allowed, scores, NEG_LARGE), axis=-1, keepdims=True)
    raised = jnp.where(allowed, jnp.exp(jnp.where(allowed, scores - peak, 0.0)), 0.0)
    totals = jnp.sum(raised, axis=-1, keepdims=True)
    return raised / jnp.where(totals > 0, totals, 1.0)


def columns(band):
    return pl.ds(band * BAND, BAND)


def piece_rows(pieces, place, mixed):
    if not mixed:
        return jnp.concatenate([piece[:, place] for piece in pieces], axis=0)
    n = pieces[0].shape[0] // 2
    found = []
    for a, b in (pieces[:2], pieces[2:]):
        for k in (slice(0, n), slice(n, 2 * n)):
            found += [a[k, place], b[k, place]]
    return jnp.concatenate(found, axis=0)


def forward_kernel(micro, per_pack, kv_bands, *refs):
    x_ref, cos_ref, sin_ref, mask_ref, *piece_refs = refs[:-4]
    qkv_ref, att_ref, n1_ref, gains_ref = refs[-4:]
    q_bands = GROUP * kv_bands
    q_refs, kv_refs = piece_refs[:4], piece_refs[4:]
    skip = q_bands // 2
    tail = pl.ds((skip + 2 * kv_bands) * BAND, LANES)
    gains = jnp.transpose(piece_rows(kv_refs, tail, False).astype(f32))
    gains_ref[...] = gains[: gains_ref.shape[0]]
    inputs = x_ref[...].astype(f32)
    scale = lax.rsqrt(jnp.mean(inputs * inputs, axis=1, keepdims=True) + EPSILON)
    n1_ref[...] = (inputs * scale * gains[:1]).astype(bf16)
    for band in range(q_bands + 2 * kv_bands):
        in_q = band < q_bands
        place = columns(band if in_q else band - q_bands + skip)
        total = product(n1_ref[...], piece_rows(q_refs if in_q else kv_refs, place, in_q))
        if band < q_bands + kv_bands:
            total = turn(total, cos_ref[...], sin_ref[...])
        qkv_ref[:, columns(band)] = total.astype(bf16)

    masks = head_masks()

    def one_pack(pack, carry):
        rows = pl.ds(pl.multiple_of(pack * per_pack, per_pack), per_pack)
        allowed = (mask_ref[pl.ds(pack, 1)] > 0.0)
        for j in range(kv_bands):
            bands = [g * kv_bands + j for g in range(GROUP)]
            stacked = stack_heads([qkv_ref[rows, columns(b)] for b in bands], masks)
            keys = qkv_ref[rows, columns(q_bands + j)]
            values = qkv_ref[rows, columns(q_bands + kv_bands + j)]
            probs = pack_probs(stacked, keys, allowed)
            mixed = product(probs.astype(bf16).reshape(-1, per_pack), values)
            for b, band in zip(bands, unstack_heads(mixed, masks, per_pack)):
                att_ref[rows, columns(b)] = band.astype(bf16)
        return carry

    lax.fori_loop(0, micro, one_pack, 0)


def pack_kernel(q_ref, k_ref, v_ref, gains_ref, o_ref, out_ref):
    heads = [
        q_ref[:, (k * GROUP + g) * HEAD : (k * GROUP + g + 1) * HEAD]
        for g in range(GROUP)
        for k in range(KV_HEADS)
    ]
    first = 0
    for piece in (
        jnp.concatenate(heads, axis=1), o_ref[...], k_ref[...], v_ref[...], gains_ref[...]
    ):
        out_ref[:, first : first + piece.shape[1]] = piece
        first += piece.shape[1]


def backward_kernel(micro, per_pack, kv_bands, *refs):
    dmb_ref, qkv_ref, cos_ref, sin_ref, mask_ref, pick_ref, *piece_refs = refs[:14]
    dqkv_ref, datt_ref = refs[-2:]
    half = pick_ref.shape[1] // 2
    everything = slice(None)
    datt = against(dmb_ref[:, :half], piece_rows(piece_refs[:4], everything, True))
    datt = datt + against(dmb_ref[:, half:], piece_rows(piece_refs[4:], everything, False))
    datt_ref[...] = against(datt.astype(bf16), pick_ref[...]).astype(bf16)
    q_bands = GROUP * kv_bands
    factor = 1.0 / math.sqrt(HEAD)
    masks = head_masks()

    def one_pack(pack, carry):
        rows = pl.ds(pl.multiple_of(pack * per_pack, per_pack), per_pack)
        allowed = (mask_ref[pl.ds(pack, 1)] > 0.0)
        cosine, sine_part = cos_ref[rows, :], -sin_ref[rows, :]
        for j in range(kv_bands):
            bands = [g * kv_bands + j for g in range(GROUP)]
            stacked = stack_heads([qkv_ref[rows, columns(b)] for b in bands], masks)
            keys = qkv_ref[rows, columns(q_bands + j)]
            values = qkv_ref[rows, columns(q_bands + kv_bands + j)]
            grads = stack_heads([datt_ref[rows, columns(b)] for b in bands], masks)
            probs = pack_probs(stacked, keys, allowed)
            dprob = against(grads, values).reshape(probs.shape)
            delta = jnp.sum(probs * dprob, axis=-1, keepdims=True)
            dscore = (probs * (dprob - delta)).astype(bf16).reshape(-1, per_pack)
            dvalue = across(probs.astype(bf16).reshape(-1, per_pack), grads)
            dkey = turn(across(dscore, stacked) * factor, cosine, sine_part)
            dquery = product(dscore, keys) * factor
            for b, band in zip(bands, unstack_heads(dquery, masks, per_pack)):
                dqkv_ref[rows, columns(b)] = turn(band, cosine, sine_part).astype(bf16)
            dqkv_ref[rows, columns(q_bands + j)] = dkey.astype(bf16)
            dqkv_ref[rows, columns(q_bands + kv_bands + j)] = dvalue.astype(bf16)
        return carry

    lax.fori_loop(0, micro, one_pack, 0)


def mlp_kernel(ff, *refs):
    weight_refs = refs[4:8]
    gu_refs, down_refs = weight_refs[:2], weight_refs[2:]
    first = pl.program_id(0) == 0
    n2_ref = jnp.where(first, refs[0][...], refs[1][...])
    dy_ref = jnp.where(first, refs[2][...], refs[3][...])
    hidden_ref, dgu_ref, *dn2_refs = refs[-4:]
    half = gu_refs[0].shape[0]
    lower, upper = slice(0, half), slice(half, 2 * half)
    both = product(n2_ref[:, lower], gu_refs[0][...]) + product(n2_ref[:, upper], gu_refs[1][...])
    gate, up = both[:, :ff], both[:, ff:]
    dhid = product(dy_ref[:, lower], down_refs[0][...])
    dhid = dhid + product(dy_ref[:, upper], down_refs[1][...])
    sig = jax.nn.sigmoid(gate)
    passed = gate * sig
    hidden_ref[...] = (passed * up).astype(bf16)
    dgu_ref[:, :ff] = (dhid * up * sig * (1.0 + gate * (1.0 - sig))).astype(bf16)
    dgu_ref[:, ff:] = (dhid * passed).astype(bf16)
    dgu = dgu_ref[...]
    dn2 = jnp.concatenate([against(dgu, gu[...]).astype(bf16) for gu in gu_refs], axis=1)
    put_by_step(dn2_refs, [dn2] * 2)


def put_by_step(refs, values):
    for k, (ref, value) in enumerate(zip(refs, values)):

        @pl.when(pl.program_id(0) == k)
        def _(ref=ref, value=value):
            ref[...] = value.astype(ref.dtype)


def shape_of(rows, columns, kind):
    return jax.ShapeDtypeStruct((rows, columns), kind)


def estimate(flops):
    return pl.CostEstimate(flops=100000000000, bytes_accessed=0, transcendentals=0)


SHORT = pl.CostEstimate(flops=10**9, bytes_accessed=0, transcendentals=0)
LIMIT = pltpu.CompilerParams(vmem_limit_bytes=56 * 1024 * 1024)
ANYWHERE = pl.BlockSpec(memory_space=pl.ANY)


def fixed(rows, columns, row=0, column=0):
    return pl.BlockSpec((rows, columns), lambda i: (row, column))


def mlp_call(first, n2, dy, weights, *earlier):
    block, width = n2[0][0].shape[0], n2[0][0].shape[1]
    rows = 4 * block
    ff = weights[-1].shape[1]

    def band(columns):
        return pl.BlockSpec((block, columns), lambda i: (first + 2 * i, 0))

    return pl.pallas_call(
        functools.partial(mlp_kernel, ff),
        grid=(2,),
        in_specs=[fixed(block, width, row) for _, row in n2 + dy]
        + [fixed(*array.shape) for array in weights]
        + [ANYWHERE] * len(earlier),
        out_specs=[band(ff), band(2 * ff), fixed(block, width), fixed(block, width)],
        out_shape=[shape_of(rows, ff, bf16), shape_of(rows, 2 * ff, bf16)]
        + [shape_of(block, width, bf16)] * 2,
        input_output_aliases={8 + k: k for k in range(len(earlier) - 1)},
        compiler_params=LIMIT,
        cost_estimate=estimate(10 * 2 * block * width * ff),
    )(*[array for array, _ in n2 + dy], *weights, *earlier)


def left_rows(refs):
    return refs[0][...] if len(refs) == 1 else jnp.concatenate([r[...] for r in refs], axis=0)


def left_parts(left, right):
    if not isinstance(left, list):
        left = [(left, 0)]
    return left, right.shape[0] // len(left), left[0][0].shape[1]


def sent_kernel(*refs):
    right_ref, _, out_ref = refs[-3:]
    out_ref[...] = across(left_rows(refs[:-3]), right_ref[...]).astype(bf16)


def sent_call(left, right, at, columns, token):
    left, count, width = left_parts(left, right)
    block = width // 4
    return pl.pallas_call(
        sent_kernel,
        grid=(2,),
        in_specs=[
            pl.BlockSpec((count, block), lambda i, row=row: (row, 2 + i)) for _, row in left
        ]
        + [fixed(right.shape[0], columns, 0, at // columns), ANYWHERE],
        out_specs=pl.BlockSpec((block, columns), lambda i: (i, 0)),
        out_shape=shape_of(2 * block, columns, bf16),
        compiler_params=LIMIT,
        cost_estimate=estimate(4 * count * block * columns),
    )(*[array for array, _ in left], right, token)


def kept_kernel(*refs):
    right_ref, got_ref, _, keep_ref, send_ref = refs[-5:]
    total = across(left_rows(refs[:-5]), right_ref[...]) + got_ref[...].astype(f32)
    put_by_step((keep_ref, send_ref), (total, total))


def kept_call(left, right, at, columns, got, token):
    left, count, width = left_parts(left, right)
    block = width // 4
    return pl.pallas_call(
        kept_kernel,
        grid=(2,),
        in_specs=[pl.BlockSpec((count, block), lambda i, row=row: (row, i)) for _, row in left]
        + [
            fixed(right.shape[0], columns, 0, at // columns),
            pl.BlockSpec((block, columns), lambda i: (i, 0)),
            ANYWHERE,
        ],
        out_specs=[fixed(block, columns)] * 2,
        out_shape=[shape_of(block, columns, f32), shape_of(block, columns, bf16)],
        compiler_params=LIMIT,
        cost_estimate=estimate(4 * count * block * columns),
    )(*[array for array, _ in left], right, got, token)


def sum_kernel(count, *refs):
    total = 0.0
    for ref in refs[:count]:
        total = total + ref[...].astype(f32)
    outs = refs[count + 1 :]
    rows = total.shape[0] // len(outs)
    for k, out in enumerate(outs):
        out[...] = total[k * rows : (k + 1) * rows].astype(out.dtype)


def sum_call(arrays, kinds, token):
    rows, columns = arrays[0].shape
    block = columns // 2 if columns % 256 == 0 else columns
    part = rows // len(kinds)
    return pl.pallas_call(
        functools.partial(sum_kernel, len(arrays)),
        grid=(columns // block,),
        in_specs=[pl.BlockSpec((rows, block), lambda i: (0, i))] * len(arrays) + [ANYWHERE],
        out_specs=[pl.BlockSpec((part, block), lambda i: (0, i))] * len(kinds),
        out_shape=[shape_of(part, columns, kind) for kind in kinds],
        compiler_params=LIMIT,
        cost_estimate=estimate(rows * columns),
    )(*arrays, token)


def norm_back(upstream, signal, gain):
    inverse = lax.rsqrt(jnp.mean(signal * signal, axis=1, keepdims=True) + EPSILON)
    weighted = upstream * gain
    mixed = jnp.mean(weighted * signal, axis=1, keepdims=True)
    return inverse * weighted - signal * (inverse * inverse * inverse) * mixed


def second_norm_kernel(*refs):
    near_ref, core_ref, x_ref, pick_ref, dy_ref, middle_ref, gain_ref, _ = refs[:8]
    dmid_ref, dmb_ref = refs[8:]
    dn2 = near_ref[...].astype(f32) + core_ref[...].astype(f32) + x_ref[...].astype(f32)
    dn2 = against(dn2.astype(bf16), pick_ref[...])
    dmid = dy_ref[...].astype(f32) + norm_back(dn2, middle_ref[...], gain_ref[...])
    dmid_ref[...] = dmid
    dmb_ref[...] = dmid.astype(bf16)


def first_norm_kernel(band, *refs):
    dqkv_ref, x_ref, gains_ref, pick_ref, dmid_ref, *piece_refs = refs[:-2]
    out_ref = refs[-1]
    dn1 = 0.0
    bands = dqkv_ref.shape[1] // band
    for k in range(bands):
        in_q = k < bands // 2
        place = pl.ds((k if in_q else k - bands // 2 + 1) * band, band)
        found = piece_rows(piece_refs[:4] if in_q else piece_refs[4:], place, in_q)
        dn1 = dn1 + against(dqkv_ref[:, pl.ds(k * band, band)], found)
    part = norm_back(dn1, x_ref[...].astype(f32), gains_ref[:1])
    high = part.astype(bf16)
    low = (part - high.astype(f32)).astype(bf16)
    out_ref[...] = dmid_ref[...] + against(high, pick_ref[...]) + against(low, pick_ref[...])


def down_kernel(hidden_ref, near_ref, far_ref, token_ref, *out_refs):
    parts = [against(hidden_ref[...], ref[...]) for ref in (near_ref, far_ref)]
    rows = jnp.concatenate(parts, axis=1)
    put_by_step(out_refs, [rows] * 4)


def down_call(hidden, near, far, token):
    rows, ff = hidden.shape
    width, block = 2 * near.shape[0], hidden.shape[0] // 4
    return pl.pallas_call(
        down_kernel,
        grid=(4,),
        in_specs=[pl.BlockSpec((block, ff), lambda i: (i, 0))]
        + [fixed(*near.shape), fixed(*far.shape), ANYWHERE],
        out_specs=[fixed(block, width)] * 4,
        out_shape=[shape_of(block, width, bf16)] * 4,
        compiler_params=LIMIT,
        cost_estimate=estimate(2 * rows * width * ff),
    )(hidden, near, far, token)


def layer_kernel(own_ref, core_ref, x_ref, pick_ref, middle_ref, token_ref, out_ref):
    total = own_ref[...].astype(f32) + core_ref[...].astype(f32) + x_ref[...].astype(f32)
    total = middle_ref[...] + against(total.astype(bf16), pick_ref[...])
    out_ref[...] = total.astype(bf16)


def join_kernel(plan, *refs):
    outs = refs[-len(plan) :]
    for out, pieces in zip(outs, plan):
        first, width = 0, out.shape[1]
        for k, column in pieces:
            rows = refs[k].shape[0]
            out[first : first + rows, :] = refs[k][:, column : column + width]
            first += rows


def pick_kernel(*refs):
    for source, out in zip(refs[:3], refs[-3:]):
        rows = lax.broadcasted_iota(jnp.int32, out.shape, 0)
        out[...] = jnp.where(rows == source[...], 1.0, 0.0).astype(bf16)


def order_kernel(count, *refs):
    pick_ref, out_ref = refs[count], refs[-1]
    n = refs[0].shape[0]
    for k, ref in enumerate(refs[:count]):
        out_ref[k * n : (k + 1) * n, :] = product(ref[...], pick_ref[...]).astype(bf16)


def two_kernel(*refs):
    gu_z, down_z, xs_y, ys_x = refs[:4]
    both_ref, xs_ref, ys_ref = refs[-3:]
    columns = gu_z.shape[1]
    both_ref[:, :columns], both_ref[:, columns:] = gu_z[...], down_z[...]
    xs_ref[...] = xs_y[...]
    ys_ref[...] = ys_x[...]


def join_call(arrays, plan, widths, token):
    outs = [
        shape_of(sum(arrays[k].shape[0] for k, _ in pieces), width, bf16)
        for pieces, width in zip(plan, widths)
    ]
    return kernel_call(
        functools.partial(join_kernel, plan), outs, estimate(0), *arrays, token=token
    )


def output_kernel(*refs):
    att_ref, pick_out_ref, x_ref, gain_ref, pick_mlp_ref, *piece_refs = refs[:13]
    rel_ref, middle_ref, n2_ref = refs[-3:]
    att = product(att_ref[...], pick_out_ref[...]).astype(bf16)
    rel_ref[...] = att
    everything = slice(None)
    left = product(att, piece_rows(piece_refs[:4], everything, True))
    right = product(att, piece_rows(piece_refs[4:], everything, False))
    middle = x_ref[...].astype(f32) + jnp.concatenate([left, right], axis=1)
    middle_ref[...] = middle
    scale = lax.rsqrt(jnp.mean(middle * middle, axis=1, keepdims=True) + EPSILON)
    n2 = (middle * scale * gain_ref[...]).astype(bf16)
    n2_ref[...] = product(n2, pick_mlp_ref[...]).astype(bf16)


def kernel_call(body, outs, cost, *args, token=(), scratch=()):
    tokens = token if isinstance(token, tuple) else (token,)
    arrays, specs = [], []

    def alone(shape, place=None):
        where = (0,) * len(shape) if place is None else (0, place)
        return pl.BlockSpec(shape, lambda i: where, pipeline_mode=pl.Buffered(1))

    for arg in args:
        array, (columns, place) = arg if isinstance(arg, tuple) else (arg, (None, None))
        arrays.append(array)
        shape = array.shape if columns is None else (array.shape[0], columns)
        specs.append(alone(shape, place))
    return pl.pallas_call(
        body,
        grid=(1,),
        out_shape=outs,
        in_specs=specs + [ANYWHERE] * len(tokens),
        out_specs=[alone(out.shape) for out in outs],
        scratch_shapes=list(scratch),
        compiler_params=LIMIT,
        cost_estimate=cost,
    )(*arrays, *tokens)


def after(array, *others):
    return lax.optimization_barrier((array,) + others)[0]


def together(*arrays):
    return lax.optimization_barrier(arrays)


def program(sizes):
    dp_n, tp_n = sizes["dp"], sizes["tensor"]
    world = dp_n * tp_n

    def swap(array, mask):
        return lax.ppermute(array, AXES, [(i, i ^ mask) for i in range(world)])

    dp_bits = [m * tp_n for m in bits_of(dp_n)]
    y_mask, z_masks = dp_bits[0], dp_bits[:0:-1]
    t_masks = bits_of(tp_n)[::-1]
    x_mask, core_mask = t_masks
    attn_masks = z_masks + [y_mask, x_mask, core_mask]
    mlp_masks = z_masks + [y_mask]

    def gather_far(own):
        if len(z_masks) == 2:
            one, two = z_masks
            return [own, swap(own, one), swap(own, two), swap(own, one ^ two)]
        held = own
        for mask in z_masks:
            held = join([held, swap(held, mask)])
        return [held]

    def finish(pair, token):
        (total,) = sum_call(pair, [f32], token)
        for mask in z_masks[:-2][::-1]:
            n = total.shape[0] // 2
            total = total[:n] + swap(total[n:].astype(bf16), mask).astype(f32)
        return total

    def per_device(
        tokens,
        lengths,
        first_gain,
        query_weight,
        key_weight,
        value_weight,
        output_weight,
        second_gain,
        gate_weight,
        up_weight,
        down_weight,
        cotangent,
    ):
        micro, per_pack, width = tokens.shape
        rows = micro * per_pack
        qw, kw = query_weight.shape[1], key_weight.shape[1]
        ff = gate_weight.shape[1]
        wide = qw + 2 * kw
        shard = query_weight.shape[0]
        dp_i, t_i = lax.axis_index("dp"), lax.axis_index("tensor")
        me = dp_i * tp_n + t_i

        x_low = tokens.reshape(rows, width)
        dy_low = cotangent.reshape(rows, width)
        half, quarter = width // 2, width // 4

        gains = jnp.pad(
            jnp.stack([first_gain, second_gain], axis=1), ((0, 0), (0, LANES - 2))
        )
        (own_attn,) = kernel_call(
            pack_kernel,
            [jax.ShapeDtypeStruct((shard, 2 * qw + 2 * kw + LANES), bf16)],
            None,
            query_weight,
            key_weight,
            value_weight,
            gains,
            output_weight,
        )
        own_gu = jnp.concatenate([gate_weight, up_weight], axis=1)
        own_down = down_weight.T
        own_mlp = jnp.concatenate([own_gu, own_down], axis=1)

        attn_source = rel_source(me, attn_masks, shard, width)
        head, lane = attn_source // HEAD, attn_source % HEAD
        out_source = (head % GROUP * KV_HEADS + head // GROUP) * HEAD + lane
        mlp_source = rel_source(dp_i, [m // tp_n for m in mlp_masks], shard * tp_n, width)

        def restore(array, pick):
            return against(array, pick)

        far = gather_far(own_attn)
        mlp_y = swap(own_mlp, y_mask)
        dy_x = swap(dy_low, x_mask)
        widths = (qw + half, half + 2 * kw + LANES)
        at = (0, widths[0])
        xs_four, ys_four = join_call(
            far, [[(k, first) for k in range(len(far))] for first in at], widths, (dy_x, mlp_y)
        )

        xs_x = swap(xs_four, x_mask)
        ys_y = swap(ys_four, y_mask)
        down_z = swap(after(own_down, xs_four), z_masks[0])
        pairs = (xs_four, xs_x, ys_four, ys_y)
        xs_eight, ys_eight = join_call(
            pairs, [[(2 * k, 0), (2 * k + 1, 0)] for k in range(2)], widths, down_z
        )

        xs_y = swap(xs_eight, y_mask)
        ys_x = swap(ys_eight, x_mask)
        gu_z = swap(after(own_gu, xs_eight), z_masks[0])
        mlp_far = swap(after(own_mlp, xs_eight), z_masks[1])
        xs_c = swap(xs_eight, core_mask)
        mlp_z, xs_far, ys_far = kernel_call(
            two_kernel,
            [
                shape_of(*own_mlp.shape, bf16),
                shape_of(*xs_y.shape, bf16),
                shape_of(*ys_x.shape, bf16),
            ],
            SHORT,
            gu_z,
            down_z,
            xs_y,
            ys_x,
            token=(xs_c, mlp_far),
        )
        ys_c = swap(after(ys_eight, mlp_z), core_mask)
        pick_attn, pick_out, pick_mlp = kernel_call(
            pick_kernel,
            [shape_of(width, width, bf16)] * 3,
            SHORT,
            *[source[None, :] for source in (attn_source, out_source, mlp_source)],
            token=mlp_z,
        )
        (x_rel,) = kernel_call(
            functools.partial(order_kernel, 1),
            [shape_of(rows, width, bf16)],
            SHORT,
            x_low,
            pick_attn,
        )

        x_pieces = [xs_eight, xs_y, xs_c, swap(xs_far, core_mask)]
        y_pieces = [ys_eight, ys_x, ys_c, swap(ys_far, core_mask)]
        q_pieces = [(piece, (qw, 0)) for piece in x_pieces]
        left_pieces = [(piece, (half, qw // half)) for piece in x_pieces]
        right_pieces = [(piece, (half, 0)) for piece in y_pieces]
        mlp_y1 = swap(mlp_z, y_mask)
        mlp_near = swap(mlp_z, z_masks[1])
        mlp_y2 = swap(mlp_far, y_mask)

        segment, position = jax.vmap(lambda own: pack_layout(own, per_pack))(lengths[:, 0])
        cosine, sine_part = rotary_tables(position, HEAD)
        row_index = jnp.arange(per_pack, dtype=jnp.int32)
        allowed = (
            (segment[:, :, None] == segment[:, None, :])
            & (row_index[None, None, :] <= row_index[None, :, None])
            & (segment < SLOTS - 1)[:, :, None]
        ).astype(f32)

        half_tables = (cosine.reshape(rows, -1), sine_part.reshape(rows, -1))
        cos_band = jnp.tile(half_tables[0], (1, BAND // half_tables[0].shape[1]))
        sin_band = jnp.tile(jnp.concatenate([-half_tables[1], half_tables[1]], axis=1), (1, 4))
        kv_bands = kw // BAND
        shapes = (micro, per_pack, kv_bands)
        cost = pl.CostEstimate(
            flops=100000000000, bytes_accessed=0, transcendentals=0
        )
        qkv, attended, n1_rel, gains_rel = kernel_call(
            functools.partial(forward_kernel, *shapes),
            [
                jax.ShapeDtypeStruct((rows, wide), bf16),
                jax.ShapeDtypeStruct((rows, qw), bf16),
                jax.ShapeDtypeStruct((rows, width), bf16),
                jax.ShapeDtypeStruct((8, width), f32),
            ],
            cost,
            x_rel,
            cos_band,
            sin_band,
            allowed,
            *q_pieces,
            *y_pieces,
        )
        g2 = restore(gains_rel[1:2].astype(bf16), pick_attn)
        (mlp_last,) = join_call((mlp_near,), [[(0, 0)]], [3 * ff], attended)
        mlp_y3 = swap(mlp_last, y_mask)
        att_rel, middle, n2_rel = kernel_call(
            output_kernel,
            [shape_of(rows, qw, bf16), shape_of(rows, width, f32), shape_of(rows, width, bf16)],
            estimate(6 * rows * width * width),
            attended,
            pick_out,
            x_low,
            g2,
            pick_mlp,
            *left_pieces,
            *right_pieces,
            token=mlp_last,
        )

        n2_x = swap(n2_rel, x_mask)
        n2_c = swap(n2_rel, core_mask)
        (dy_near,) = kernel_call(
            functools.partial(order_kernel, 2),
            [shape_of(2 * rows, width, bf16)],
            estimate(0),
            dy_low,
            dy_x,
            pick_mlp,
            token=n2_rel,
        )
        dy_c = swap(dy_near, core_mask)
        near_parts = (own_mlp, mlp_z, mlp_far, mlp_last)
        far_parts = (mlp_y, mlp_y1, mlp_y2, mlp_y3)
        for mask in z_masks[2:]:
            near_parts = near_parts + (swap(join(near_parts), mask),)
            far_parts = far_parts + (swap(near_parts[-1], y_mask),)

        def assemble(parts, token):
            plan = [[(k, 0) for k in range(len(parts))], [(k, 2 * ff) for k in range(len(parts))]]
            return join_call(parts, plan, (2 * ff, ff), token)

        gu_near, down_near = assemble(near_parts, dy_near)
        (n2_f,) = join_call((n2_x,), [[(0, 0)]], [width], (mlp_y2,) + far_parts[-1:] + (gu_near,))
        n2_xc = swap(n2_f, core_mask)
        gu_far, down_far = assemble(far_parts, n2_f)
        weights = (gu_near, gu_far, down_near, down_far)
        n2_all = [(n2_rel, 0), (n2_x, 0), (n2_c, 0), (n2_xc, 0)]
        dy_all = [(dy_near, 0), (dy_near, 1), (dy_c, 0), (dy_c, 1)]
        weights = (gu_near, gu_far, down_near, down_far)
        *grown, far_own, far_send = mlp_call(
            1, n2_all[1::2], dy_all[1::2], weights, gu_far
        )
        far_c = swap(far_send, core_mask)
        (dn2_sum,) = sum_call([far_own, far_c], [bf16], far_own)
        dn2_x = swap(dn2_sum, x_mask)
        hidden, dgu, near_own, near_send = mlp_call(
            0, n2_all[::2], dy_all[::2], weights, *grown, dn2_sum
        )
        near_c = swap(near_send, core_mask)
        down_b = sent_call(dy_all, hidden, 0, ff, near_own)
        down_got = swap(down_b, y_mask)

        dmid, dmb = kernel_call(
            second_norm_kernel,
            [shape_of(rows, width, f32), shape_of(rows, width, bf16)],
            estimate(4 * rows * width * width),
            near_own,
            near_c,
            dn2_x,
            pick_mlp,
            dy_low,
            middle,
            g2,
            token=down_b,
        )
        (dqkv,) = kernel_call(
            functools.partial(backward_kernel, *shapes),
            [shape_of(rows, wide, bf16)],
            cost,
            dmb,
            qkv,
            cos_band,
            sin_band,
            allowed,
            pick_out,
            *left_pieces,
            *right_pieces,
            scratch=[pltpu.VMEM((rows, qw), bf16)],
        )
        qkv_b = sent_call(n1_rel, dqkv, 0, wide, dqkv)
        qkv_c = swap(qkv_b, core_mask)
        gate_b = sent_call(n2_all, dgu, 0, ff, qkv_b)
        gate_got = swap(gate_b, y_mask)
        far_mask, near_mask = z_masks[-1], z_masks[-2]
        step = [f32, bf16]

        def onward(pair, got, mask, token):
            pair = sum_call([pair[0], got], step, token)
            return pair, swap(pair[1], mask)

        qkv_k = kept_call(n1_rel, dqkv, 0, wide, qkv_c, gate_b)
        qkv_got = swap(qkv_k[1], x_mask)
        down_k = kept_call(dy_all, hidden, 0, ff, down_got, qkv_k[0])
        down_got = swap(down_k[1], far_mask)
        up_b = sent_call(n2_all, dgu, ff, ff, down_k[0])
        up_got = swap(up_b, y_mask)
        gate_k = kept_call(n2_all, dgu, 0, ff, gate_got, up_b)
        gate_got = swap(gate_k[1], far_mask)
        (input_grad,) = kernel_call(
            functools.partial(first_norm_kernel, 2 * BAND),
            [shape_of(rows, width, f32)],
            estimate(2 * rows * width * (wide + 2 * width)),
            dqkv,
            x_rel,
            gains_rel,
            pick_attn,
            dmid,
            *q_pieces,
            *y_pieces,
            token=gate_k[0],
        )
        down_k, down_got = onward(down_k, down_got, near_mask, input_grad)
        gate_k, gate_got = onward(gate_k, gate_got, near_mask, down_k[0])
        up_k = kept_call(n2_all, dgu, ff, ff, up_got, gate_k[0])
        up_got = swap(up_k[1], far_mask)
        og_b = sent_call(att_rel, dmb, 0, width, up_k[0])
        og_c = swap(og_b, core_mask)
        down_grad = finish([down_k[0], down_got], og_b)
        qkv_k, qkv_got = onward(qkv_k, qkv_got, y_mask, down_grad)
        og = kept_call(att_rel, dmb, 0, width, og_c, qkv_k[0])
        og_got = swap(og[1], x_mask)
        gate_grad = finish([gate_k[0], gate_got], og[0])
        up_k, up_got = onward(up_k, up_got, near_mask, gate_grad)
        lay = down_call(hidden, *weights[2:], up_k[0])
        lay_f = swap(lay[3], core_mask)
        og, og_got = onward(og, og_got, y_mask, lay[0])
        (lay_s,) = sum_call([lay[1], lay_f], [bf16], og[0])
        lay_x = swap(lay_s, x_mask)
        qkv_k, qkv_got = onward(qkv_k, qkv_got, far_mask, lay_s)
        og, og_got = onward(og, og_got, far_mask, qkv_k[0])
        lay_c = swap(after(lay[2], og[0]), core_mask)
        up_grad = finish([up_k[0], up_got], og[0])
        qkv_k, qkv_got = onward(qkv_k, qkv_got, near_mask, up_grad)
        og, og_got = onward(og, og_got, near_mask, qkv_k[0])
        (layer_out,) = kernel_call(
            layer_kernel,
            [shape_of(rows, width, bf16)],
            estimate(2 * rows * width * width),
            lay[0],
            lay_c,
            lay_x,
            pick_mlp,
            middle,
            token=og[0],
        )
        qkv_grad = finish([qkv_k[0], qkv_got], layer_out)
        output_grad = finish([og[0], og_got], qkv_grad)
        q_grad, kv_grad = qkv_grad[:, :qw], qkv_grad[:, qw:]
        down_grad = down_grad.T

        first = jnp.sum(own_attn[:, :qw].astype(f32) * q_grad, axis=1)
        own_kv = own_attn[:, qw + width : qw + width + 2 * kw].astype(f32)
        first = first + jnp.sum(own_kv * kv_grad, axis=1)
        first_gain_grad = first / first_gain.astype(f32)
        second = jnp.sum(
            gate_weight.astype(f32) * gate_grad + up_weight.astype(f32) * up_grad, axis=1
        )
        for mask in t_masks:
            second = second + swap(second, mask)
        second = lax.dynamic_slice(second, (t_i * shard,), (shard,))
        second_gain_grad = second / second_gain.astype(f32)

        return (
            layer_out.reshape(tokens.shape),
            input_grad.reshape(tokens.shape),
            first_gain_grad,
            q_grad.reshape(shard, GROUP, KV_HEADS, HEAD).swapaxes(1, 2).reshape(shard, qw),
            kv_grad[:, :kw],
            kv_grad[:, kw:],
            output_grad,
            second_gain_grad,
            gate_grad,
            up_grad,
            down_grad,
        )

    return per_device


def solution(mesh):
    rows = P(None, AXES, None)
    split = P(AXES, None)
    placed = (
        rows,
        rows,
        P(AXES),
        split,
        split,
        split,
        split,
        P(AXES),
        P("dp", "tensor"),
        P("dp", "tensor"),
        P("tensor", "dp"),
        rows,
    )
    return jax.shard_map(
        program(dict(mesh.shape)),
        mesh=mesh,
        in_specs=placed,
        out_specs=(
            rows,
            rows,
            P(AXES),
            split,
            split,
            split,
            split,
            P(AXES),
            P("dp", "tensor"),
            P("dp", "tensor"),
            P("tensor", "dp"),
        ),
        check_vma=False,
    )
```

```python
import functools
import math

import jax
import jax.numpy as jnp
from jax import lax
from jax.experimental import pallas as pl
from jax.experimental.pallas import tpu as pltpu
from jax.sharding import PartitionSpec as P

HEADS = 16
KV_HEADS = 8
HEAD = 96
SLOTS = 6
GROUP = HEADS // KV_HEADS
LANES = 128

EPSILON = 1e-05
ROPE_BASE = 100000.0
NEG_LARGE = -1e30
AXES = ("dp", "tensor")
bf16 = jnp.bfloat16
f32 = jnp.float32


def pack_layout(seq_lengths, row_count):
    seq_ends = jnp.cumsum(seq_lengths)
    seq_starts = seq_ends - seq_lengths
    row_index = jnp.arange(row_count, dtype=jnp.int32)
    segment = jnp.sum((row_index[:, None] >= seq_ends[None, :]).astype(jnp.int32), axis=1)
    owner_hot = segment[:, None] == jnp.arange(seq_lengths.shape[0], dtype=jnp.int32)[None, :]
    position = row_index - jnp.sum(jnp.where(owner_hot, seq_starts[None, :], 0), axis=1)
    return (segment, position)


def rotary_tables(position, head_size):
    half_size = head_size // 2
    freq_index = jnp.arange(half_size, dtype=f32)
    inverse = jnp.exp(freq_index * (-2.0 / head_size) * math.log(ROPE_BASE))
    angles = position.astype(f32)[..., None] * inverse
    return (jnp.cos(angles), jnp.sin(angles))


def product(left_side, right_side):
    return jnp.dot(left_side, right_side, preferred_element_type=f32)


def across(left_side, right_side):
    return lax.dot_general(
        left_side, right_side, (((0,), (0,)), ((), ())), preferred_element_type=f32
    )


def against(left_side, right_side):
    return lax.dot_general(
        left_side, right_side, (((1,), (1,)), ((), ())), preferred_element_type=f32
    )


def bits_of(size):
    return [1 << k for k in range(size.bit_length() - 1)]


def rel_source(me, masks, block, count):
    place = jnp.arange(count, dtype=jnp.int32)
    step = place // block
    delta = jnp.zeros_like(step)
    for k, mask in enumerate(masks):
        delta = delta + ((step >> k) & 1) * mask
    return (me ^ delta) * block + place % block


def join(parts):
    return parts[0] if len(parts) == 1 else jnp.concatenate(parts, axis=0)


BAND = 4 * HEAD


def turn(array, cosine, sine_part):
    lane = lax.broadcasted_iota(jnp.int32, array.shape, 1)
    swapped = jnp.where(
        lane % HEAD < HEAD // 2,
        pltpu.roll(array, BAND - HEAD // 2, 1),
        pltpu.roll(array, HEAD // 2, 1),
    )
    return array * cosine + swapped * sine_part


def head_masks():
    lane = lax.broadcasted_iota(jnp.int32, (1, BAND), 1)
    return [jnp.where(lane // HEAD == h, 1.0, 0.0) for h in range(4)]


def stack_heads(bands, masks):
    return jnp.concatenate([band * mask.astype(bf16) for band in bands for mask in masks], axis=0)


def unstack_heads(stacked, masks, per_pack):
    found = []
    for g in range(GROUP):
        total = 0.0
        for h in range(4):
            first = (g * 4 + h) * per_pack
            total = total + stacked[first : first + per_pack] * masks[h]
        found.append(total)
    return found


def pack_probs(stacked, keys, allowed):
    per_pack = keys.shape[0]
    scores = against(stacked, keys) * (1.0 / math.sqrt(HEAD))
    scores = scores.reshape(-1, per_pack, per_pack)
    peak = jnp.max(jnp.where(allowed, scores, NEG_LARGE), axis=-1, keepdims=True)
    raised = jnp.where(allowed, jnp.exp(jnp.where(allowed, scores - peak, 0.0)), 0.0)
    totals = jnp.sum(raised, axis=-1, keepdims=True)
    return raised / jnp.where(totals > 0, totals, 1.0)


def columns(band):
    return pl.ds(band * BAND, BAND)


def piece_rows(pieces, place, mixed):
    if not mixed:
        return jnp.concatenate([piece[:, place] for piece in pieces], axis=0)
    n = pieces[0].shape[0] // 2
    found = []
    for a, b in (pieces[:2], pieces[2:]):
        for k in (slice(0, n), slice(n, 2 * n)):
            found += [a[k, place], b[k, place]]
    return jnp.concatenate(found, axis=0)


def forward_kernel(micro, per_pack, kv_bands, *refs):
    x_ref, cos_ref, sin_ref, mask_ref, *piece_refs = refs[:-4]
    qkv_ref, att_ref, n1_ref, gains_ref = refs[-4:]
    q_bands = GROUP * kv_bands
    q_refs, kv_refs = piece_refs[:4], piece_refs[4:]
    skip = q_bands // 2
    tail = pl.ds((skip + 2 * kv_bands) * BAND, LANES)
    gains = jnp.transpose(piece_rows(kv_refs, tail, False).astype(f32))
    gains_ref[...] = gains[: gains_ref.shape[0]]
    inputs = x_ref[...].astype(f32)
    scale = lax.rsqrt(jnp.mean(inputs * inputs, axis=1, keepdims=True) + EPSILON)
    n1_ref[...] = (inputs * scale * gains[:1]).astype(bf16)
    for band in range(q_bands + 2 * kv_bands):
        in_q = band < q_bands
        place = columns(band if in_q else band - q_bands + skip)
        total = product(n1_ref[...], piece_rows(q_refs if in_q else kv_refs, place, in_q))
        if band < q_bands + kv_bands:
            total = turn(total, cos_ref[...], sin_ref[...])
        qkv_ref[:, columns(band)] = total.astype(bf16)

    masks = head_masks()

    def one_pack(pack, carry):
        rows = pl.ds(pl.multiple_of(pack * per_pack, per_pack), per_pack)
        allowed = (mask_ref[pl.ds(pack, 1)] > 0.0)
        for j in range(kv_bands):
            bands = [g * kv_bands + j for g in range(GROUP)]
            stacked = stack_heads([qkv_ref[rows, columns(b)] for b in bands], masks)
            keys = qkv_ref[rows, columns(q_bands + j)]
            values = qkv_ref[rows, columns(q_bands + kv_bands + j)]
            probs = pack_probs(stacked, keys, allowed)
            mixed = product(probs.astype(bf16).reshape(-1, per_pack), values)
            for b, band in zip(bands, unstack_heads(mixed, masks, per_pack)):
                att_ref[rows, columns(b)] = band.astype(bf16)
        return carry

    lax.fori_loop(0, micro, one_pack, 0)


def pack_kernel(q_ref, k_ref, v_ref, gains_ref, o_ref, out_ref):
    heads = [
        q_ref[:, (k * GROUP + g) * HEAD : (k * GROUP + g + 1) * HEAD]
        for g in range(GROUP)
        for k in range(KV_HEADS)
    ]
    first = 0
    for piece in (
        jnp.concatenate(heads, axis=1), o_ref[...], k_ref[...], v_ref[...], gains_ref[...]
    ):
        out_ref[:, first : first + piece.shape[1]] = piece
        first += piece.shape[1]


def backward_kernel(micro, per_pack, kv_bands, *refs):
    dmb_ref, qkv_ref, cos_ref, sin_ref, mask_ref, pick_ref, *piece_refs = refs[:14]
    dqkv_ref, datt_ref = refs[-2:]
    half = pick_ref.shape[1] // 2
    everything = slice(None)
    datt = against(dmb_ref[:, :half], piece_rows(piece_refs[:4], everything, True))
    datt = datt + against(dmb_ref[:, half:], piece_rows(piece_refs[4:], everything, False))
    datt_ref[...] = against(datt.astype(bf16), pick_ref[...]).astype(bf16)
    q_bands = GROUP * kv_bands
    factor = 1.0 / math.sqrt(HEAD)
    masks = head_masks()

    def one_pack(pack, carry):
        rows = pl.ds(pl.multiple_of(pack * per_pack, per_pack), per_pack)
        allowed = (mask_ref[pl.ds(pack, 1)] > 0.0)
        cosine, sine_part = cos_ref[rows, :], -sin_ref[rows, :]
        for j in range(kv_bands):
            bands = [g * kv_bands + j for g in range(GROUP)]
            stacked = stack_heads([qkv_ref[rows, columns(b)] for b in bands], masks)
            keys = qkv_ref[rows, columns(q_bands + j)]
            values = qkv_ref[rows, columns(q_bands + kv_bands + j)]
            grads = stack_heads([datt_ref[rows, columns(b)] for b in bands], masks)
            probs = pack_probs(stacked, keys, allowed)
            dprob = against(grads, values).reshape(probs.shape)
            delta = jnp.sum(probs * dprob, axis=-1, keepdims=True)
            dscore = (probs * (dprob - delta)).astype(bf16).reshape(-1, per_pack)
            dvalue = across(probs.astype(bf16).reshape(-1, per_pack), grads)
            dkey = turn(across(dscore, stacked) * factor, cosine, sine_part)
            dquery = product(dscore, keys) * factor
            for b, band in zip(bands, unstack_heads(dquery, masks, per_pack)):
                dqkv_ref[rows, columns(b)] = turn(band, cosine, sine_part).astype(bf16)
            dqkv_ref[rows, columns(q_bands + j)] = dkey.astype(bf16)
            dqkv_ref[rows, columns(q_bands + kv_bands + j)] = dvalue.astype(bf16)
        return carry

    lax.fori_loop(0, micro, one_pack, 0)


def mlp_kernel(ff, *refs):
    weight_refs = refs[4:8]
    gu_refs, down_refs = weight_refs[:2], weight_refs[2:]
    first = pl.program_id(0) == 0
    n2_ref = jnp.where(first, refs[0][...], refs[1][...])
    dy_ref = jnp.where(first, refs[2][...], refs[3][...])
    hidden_ref, dgu_ref, *dn2_refs = refs[-4:]
    half = gu_refs[0].shape[0]
    lower, upper = slice(0, half), slice(half, 2 * half)
    both = product(n2_ref[:, lower], gu_refs[0][...]) + product(n2_ref[:, upper], gu_refs[1][...])
    gate, up = both[:, :ff], both[:, ff:]
    dhid = product(dy_ref[:, lower], down_refs[0][...])
    dhid = dhid + product(dy_ref[:, upper], down_refs[1][...])
    sig = jax.nn.sigmoid(gate)
    passed = gate * sig
    hidden_ref[...] = (passed * up).astype(bf16)
    dgu_ref[:, :ff] = (dhid * up * sig * (1.0 + gate * (1.0 - sig))).astype(bf16)
    dgu_ref[:, ff:] = (dhid * passed).astype(bf16)
    dgu = dgu_ref[...]
    dn2 = jnp.concatenate([against(dgu, gu[...]).astype(bf16) for gu in gu_refs], axis=1)
    put_by_step(dn2_refs, [dn2] * 2)


def put_by_step(refs, values):
    for k, (ref, value) in enumerate(zip(refs, values)):

        @pl.when(pl.program_id(0) == k)
        def _(ref=ref, value=value):
            ref[...] = value.astype(ref.dtype)


def shape_of(rows, columns, kind):
    return jax.ShapeDtypeStruct((rows, columns), kind)


def estimate(flops):
    return pl.CostEstimate(flops=100000000000, bytes_accessed=0, transcendentals=0)


SHORT = pl.CostEstimate(flops=10**9, bytes_accessed=0, transcendentals=0)
LIMIT = pltpu.CompilerParams(vmem_limit_bytes=56 * 1024 * 1024)
ANYWHERE = pl.BlockSpec(memory_space=pl.ANY)


def fixed(rows, columns, row=0, column=0):
    return pl.BlockSpec((rows, columns), lambda i: (row, column))


def mlp_call(first, n2, dy, weights, *earlier):
    block, width = n2[0][0].shape[0], n2[0][0].shape[1]
    rows = 4 * block
    ff = weights[-1].shape[1]

    def band(columns):
        return pl.BlockSpec((block, columns), lambda i: (first + 2 * i, 0))

    return pl.pallas_call(
        functools.partial(mlp_kernel, ff),
        grid=(2,),
        in_specs=[fixed(block, width, row) for _, row in n2 + dy]
        + [fixed(*array.shape) for array in weights]
        + [ANYWHERE] * len(earlier),
        out_specs=[band(ff), band(2 * ff), fixed(block, width), fixed(block, width)],
        out_shape=[shape_of(rows, ff, bf16), shape_of(rows, 2 * ff, bf16)]
        + [shape_of(block, width, bf16)] * 2,
        input_output_aliases={8 + k: k for k in range(len(earlier) - 1)},
        compiler_params=LIMIT,
        cost_estimate=estimate(10 * 2 * block * width * ff),
    )(*[array for array, _ in n2 + dy], *weights, *earlier)


def left_rows(refs):
    return refs[0][...] if len(refs) == 1 else jnp.concatenate([r[...] for r in refs], axis=0)


def left_parts(left, right):
    if not isinstance(left, list):
        left = [(left, 0)]
    return left, right.shape[0] // len(left), left[0][0].shape[1]


def sent_kernel(*refs):
    right_ref, _, out_ref = refs[-3:]
    out_ref[...] = across(left_rows(refs[:-3]), right_ref[...]).astype(bf16)


def sent_call(left, right, at, columns, token):
    left, count, width = left_parts(left, right)
    block = width // 4
    return pl.pallas_call(
        sent_kernel,
        grid=(2,),
        in_specs=[
            pl.BlockSpec((count, block), lambda i, row=row: (row, 2 + i)) for _, row in left
        ]
        + [fixed(right.shape[0], columns, 0, at // columns), ANYWHERE],
        out_specs=pl.BlockSpec((block, columns), lambda i: (i, 0)),
        out_shape=shape_of(2 * block, columns, bf16),
        compiler_params=LIMIT,
        cost_estimate=estimate(4 * count * block * columns),
    )(*[array for array, _ in left], right, token)


def kept_kernel(*refs):
    right_ref, got_ref, _, keep_ref, send_ref = refs[-5:]
    total = across(left_rows(refs[:-5]), right_ref[...]) + got_ref[...].astype(f32)
    put_by_step((keep_ref, send_ref), (total, total))


def kept_call(left, right, at, columns, got, token):
    left, count, width = left_parts(left, right)
    block = width // 4
    return pl.pallas_call(
        kept_kernel,
        grid=(2,),
        in_specs=[pl.BlockSpec((count, block), lambda i, row=row: (row, i)) for _, row in left]
        + [
            fixed(right.shape[0], columns, 0, at // columns),
            pl.BlockSpec((block, columns), lambda i: (i, 0)),
            ANYWHERE,
        ],
        out_specs=[fixed(block, columns)] * 2,
        out_shape=[shape_of(block, columns, f32), shape_of(block, columns, bf16)],
        compiler_params=LIMIT,
        cost_estimate=estimate(4 * count * block * columns),
    )(*[array for array, _ in left], right, got, token)


def sum_kernel(count, *refs):
    total = 0.0
    for ref in refs[:count]:
        total = total + ref[...].astype(f32)
    outs = refs[count + 1 :]
    rows = total.shape[0] // len(outs)
    for k, out in enumerate(outs):
        out[...] = total[k * rows : (k + 1) * rows].astype(out.dtype)


def sum_call(arrays, kinds, token):
    rows, columns = arrays[0].shape
    block = columns // 2 if columns % 256 == 0 else columns
    part = rows // len(kinds)
    return pl.pallas_call(
        functools.partial(sum_kernel, len(arrays)),
        grid=(columns // block,),
        in_specs=[pl.BlockSpec((rows, block), lambda i: (0, i))] * len(arrays) + [ANYWHERE],
        out_specs=[pl.BlockSpec((part, block), lambda i: (0, i))] * len(kinds),
        out_shape=[shape_of(part, columns, kind) for kind in kinds],
        compiler_params=LIMIT,
        cost_estimate=estimate(rows * columns),
    )(*arrays, token)


def norm_back(upstream, signal, gain):
    inverse = lax.rsqrt(jnp.mean(signal * signal, axis=1, keepdims=True) + EPSILON)
    weighted = upstream * gain
    mixed = jnp.mean(weighted * signal, axis=1, keepdims=True)
    return inverse * weighted - signal * (inverse * inverse * inverse) * mixed


def second_norm_kernel(*refs):
    near_ref, core_ref, x_ref, pick_ref, dy_ref, middle_ref, gain_ref, _ = refs[:8]
    dmid_ref, dmb_ref = refs[8:]
    dn2 = near_ref[...].astype(f32) + core_ref[...].astype(f32) + x_ref[...].astype(f32)
    dn2 = against(dn2.astype(bf16), pick_ref[...])
    dmid = dy_ref[...].astype(f32) + norm_back(dn2, middle_ref[...], gain_ref[...])
    dmid_ref[...] = dmid
    dmb_ref[...] = dmid.astype(bf16)


def first_norm_kernel(band, *refs):
    dqkv_ref, x_ref, gains_ref, pick_ref, dmid_ref, *piece_refs = refs[:-2]
    out_ref = refs[-1]
    dn1 = 0.0
    bands = dqkv_ref.shape[1] // band
    for k in range(bands):
        in_q = k < bands // 2
        place = pl.ds((k if in_q else k - bands // 2 + 1) * band, band)
        found = piece_rows(piece_refs[:4] if in_q else piece_refs[4:], place, in_q)
        dn1 = dn1 + against(dqkv_ref[:, pl.ds(k * band, band)], found)
    part = norm_back(dn1, x_ref[...].astype(f32), gains_ref[:1])
    high = part.astype(bf16)
    low = (part - high.astype(f32)).astype(bf16)
    out_ref[...] = dmid_ref[...] + against(high, pick_ref[...]) + against(low, pick_ref[...])


def down_kernel(hidden_ref, near_ref, far_ref, token_ref, *out_refs):
    parts = [against(hidden_ref[...], ref[...]) for ref in (near_ref, far_ref)]
    rows = jnp.concatenate(parts, axis=1)
    put_by_step(out_refs, [rows] * 4)


def down_call(hidden, near, far, token):
    rows, ff = hidden.shape
    width, block = 2 * near.shape[0], hidden.shape[0] // 4
    return pl.pallas_call(
        down_kernel,
        grid=(4,),
        in_specs=[pl.BlockSpec((block, ff), lambda i: (i, 0))]
        + [fixed(*near.shape), fixed(*far.shape), ANYWHERE],
        out_specs=[fixed(block, width)] * 4,
        out_shape=[shape_of(block, width, bf16)] * 4,
        compiler_params=LIMIT,
        cost_estimate=estimate(2 * rows * width * ff),
    )(hidden, near, far, token)


def layer_kernel(own_ref, core_ref, x_ref, pick_ref, middle_ref, token_ref, out_ref):
    total = own_ref[...].astype(f32) + core_ref[...].astype(f32) + x_ref[...].astype(f32)
    total = middle_ref[...] + against(total.astype(bf16), pick_ref[...])
    out_ref[...] = total.astype(bf16)


def join_kernel(plan, *refs):
    outs = refs[-len(plan) :]
    for out, pieces in zip(outs, plan):
        first, width = 0, out.shape[1]
        for k, column in pieces:
            rows = refs[k].shape[0]
            out[first : first + rows, :] = refs[k][:, column : column + width]
            first += rows


def pick_kernel(*refs):
    for source, out in zip(refs[:3], refs[-3:]):
        rows = lax.broadcasted_iota(jnp.int32, out.shape, 0)
        out[...] = jnp.where(rows == source[...], 1.0, 0.0).astype(bf16)


def order_kernel(count, *refs):
    pick_ref, out_ref = refs[count], refs[-1]
    n = refs[0].shape[0]
    for k, ref in enumerate(refs[:count]):
        out_ref[k * n : (k + 1) * n, :] = product(ref[...], pick_ref[...]).astype(bf16)


def two_kernel(*refs):
    gu_z, down_z, xs_y, ys_x = refs[:4]
    both_ref, xs_ref, ys_ref = refs[-3:]
    columns = gu_z.shape[1]
    both_ref[:, :columns], both_ref[:, columns:] = gu_z[...], down_z[...]
    xs_ref[...] = xs_y[...]
    ys_ref[...] = ys_x[...]


def join_call(arrays, plan, widths, token):
    outs = [
        shape_of(sum(arrays[k].shape[0] for k, _ in pieces), width, bf16)
        for pieces, width in zip(plan, widths)
    ]
    return kernel_call(
        functools.partial(join_kernel, plan), outs, estimate(0), *arrays, token=token
    )


def output_kernel(*refs):
    att_ref, pick_out_ref, x_ref, gain_ref, pick_mlp_ref, *piece_refs = refs[:13]
    rel_ref, middle_ref, n2_ref = refs[-3:]
    att = product(att_ref[...], pick_out_ref[...]).astype(bf16)
    rel_ref[...] = att
    everything = slice(None)
    left = product(att, piece_rows(piece_refs[:4], everything, True))
    right = product(att, piece_rows(piece_refs[4:], everything, False))
    middle = x_ref[...].astype(f32) + jnp.concatenate([left, right], axis=1)
    middle_ref[...] = middle
    scale = lax.rsqrt(jnp.mean(middle * middle, axis=1, keepdims=True) + EPSILON)
    n2 = (middle * scale * gain_ref[...]).astype(bf16)
    n2_ref[...] = product(n2, pick_mlp_ref[...]).astype(bf16)


def kernel_call(body, outs, cost, *args, token=(), scratch=()):
    tokens = token if isinstance(token, tuple) else (token,)
    arrays, specs = [], []

    def alone(shape, place=None):
        where = (0,) * len(shape) if place is None else (0, place)
        return pl.BlockSpec(shape, lambda i: where, pipeline_mode=pl.Buffered(1))

    for arg in args:
        array, (columns, place) = arg if isinstance(arg, tuple) else (arg, (None, None))
        arrays.append(array)
        shape = array.shape if columns is None else (array.shape[0], columns)
        specs.append(alone(shape, place))
    return pl.pallas_call(
        body,
        grid=(1,),
        out_shape=outs,
        in_specs=specs + [ANYWHERE] * len(tokens),
        out_specs=[alone(out.shape) for out in outs],
        scratch_shapes=list(scratch),
        compiler_params=LIMIT,
        cost_estimate=cost,
    )(*arrays, *tokens)


def after(array, *others):
    return lax.optimization_barrier((array,) + others)[0]


def together(*arrays):
    return lax.optimization_barrier(arrays)


def program(sizes):
    dp_n, tp_n = sizes["dp"], sizes["tensor"]
    world = dp_n * tp_n

    def swap(array, mask):
        return lax.ppermute(array, AXES, [(i, i ^ mask) for i in range(world)])

    dp_bits = [m * tp_n for m in bits_of(dp_n)]
    y_mask, z_masks = dp_bits[0], dp_bits[:0:-1]
    t_masks = bits_of(tp_n)[::-1]
    x_mask, core_mask = t_masks
    attn_masks = z_masks + [y_mask, x_mask, core_mask]
    mlp_masks = z_masks + [y_mask]

    def gather_far(own):
        if len(z_masks) == 2:
            one, two = z_masks
            return [own, swap(own, one), swap(own, two), swap(own, one ^ two)]
        held = own
        for mask in z_masks:
            held = join([held, swap(held, mask)])
        return [held]

    def finish(pair, token):
        (total,) = sum_call(pair, [f32], token)
        for mask in z_masks[:-2][::-1]:
            n = total.shape[0] // 2
            total = total[:n] + swap(total[n:].astype(bf16), mask).astype(f32)
        return total

    def per_device(
        tokens,
        lengths,
        first_gain,
        query_weight,
        key_weight,
        value_weight,
        output_weight,
        second_gain,
        gate_weight,
        up_weight,
        down_weight,
        cotangent,
    ):
        micro, per_pack, width = tokens.shape
        rows = micro * per_pack
        qw, kw = query_weight.shape[1], key_weight.shape[1]
        ff = gate_weight.shape[1]
        wide = qw + 2 * kw
        shard = query_weight.shape[0]
        dp_i, t_i = lax.axis_index("dp"), lax.axis_index("tensor")
        me = dp_i * tp_n + t_i

        x_low = tokens.reshape(rows, width)
        dy_low = cotangent.reshape(rows, width)
        half, quarter = width // 2, width // 4

        gains = jnp.pad(
            jnp.stack([first_gain, second_gain], axis=1), ((0, 0), (0, LANES - 2))
        )
        (own_attn,) = kernel_call(
            pack_kernel,
            [jax.ShapeDtypeStruct((shard, 2 * qw + 2 * kw + LANES), bf16)],
            None,
            query_weight,
            key_weight,
            value_weight,
            gains,
            output_weight,
        )
        own_gu = jnp.concatenate([gate_weight, up_weight], axis=1)
        own_down = down_weight.T
        own_mlp = jnp.concatenate([own_gu, own_down], axis=1)

        attn_source = rel_source(me, attn_masks, shard, width)
        head, lane = attn_source // HEAD, attn_source % HEAD
        out_source = (head % GROUP * KV_HEADS + head // GROUP) * HEAD + lane
        mlp_source = rel_source(dp_i, [m // tp_n for m in mlp_masks], shard * tp_n, width)

        def restore(array, pick):
            return against(array, pick)

        far = gather_far(own_attn)
        mlp_y = swap(own_mlp, y_mask)
        dy_x = swap(dy_low, x_mask)
        widths = (qw + half, half + 2 * kw + LANES)
        at = (0, widths[0])
        xs_four, ys_four = join_call(
            far, [[(k, first) for k in range(len(far))] for first in at], widths, (dy_x, mlp_y)
        )

        xs_x = swap(xs_four, x_mask)
        ys_y = swap(ys_four, y_mask)
        down_z = swap(after(own_down, xs_four), z_masks[0])
        pairs = (xs_four, xs_x, ys_four, ys_y)
        xs_eight, ys_eight = join_call(
            pairs, [[(2 * k, 0), (2 * k + 1, 0)] for k in range(2)], widths, down_z
        )

        xs_y = swap(xs_eight, y_mask)
        ys_x = swap(ys_eight, x_mask)
        gu_z = swap(after(own_gu, xs_eight), z_masks[0])
        mlp_far = swap(after(own_mlp, xs_eight), z_masks[1])
        xs_c = swap(xs_eight, core_mask)
        mlp_z, xs_far, ys_far = kernel_call(
            two_kernel,
            [
                shape_of(*own_mlp.shape, bf16),
                shape_of(*xs_y.shape, bf16),
                shape_of(*ys_x.shape, bf16),
            ],
            SHORT,
            gu_z,
            down_z,
            xs_y,
            ys_x,
            token=(xs_c, mlp_far),
        )
        ys_c = swap(after(ys_eight, mlp_z), core_mask)
        pick_attn, pick_out, pick_mlp = kernel_call(
            pick_kernel,
            [shape_of(width, width, bf16)] * 3,
            SHORT,
            *[source[None, :] for source in (attn_source, out_source, mlp_source)],
            token=mlp_z,
        )
        (x_rel,) = kernel_call(
            functools.partial(order_kernel, 1),
            [shape_of(rows, width, bf16)],
            SHORT,
            x_low,
            pick_attn,
        )

        x_pieces = [xs_eight, xs_y, xs_c, swap(xs_far, core_mask)]
        y_pieces = [ys_eight, ys_x, ys_c, swap(ys_far, core_mask)]
        q_pieces = [(piece, (qw, 0)) for piece in x_pieces]
        left_pieces = [(piece, (half, qw // half)) for piece in x_pieces]
        right_pieces = [(piece, (half, 0)) for piece in y_pieces]
        mlp_y1 = swap(mlp_z, y_mask)
        mlp_near = swap(mlp_z, z_masks[1])
        mlp_y2 = swap(mlp_far, y_mask)

        segment, position = jax.vmap(lambda own: pack_layout(own, per_pack))(lengths[:, 0])
        cosine, sine_part = rotary_tables(position, HEAD)
        row_index = jnp.arange(per_pack, dtype=jnp.int32)
        allowed = (
            (segment[:, :, None] == segment[:, None, :])
            & (row_index[None, None, :] <= row_index[None, :, None])
            & (segment < SLOTS - 1)[:, :, None]
        ).astype(f32)

        half_tables = (cosine.reshape(rows, -1), sine_part.reshape(rows, -1))
        cos_band = jnp.tile(half_tables[0], (1, BAND // half_tables[0].shape[1]))
        sin_band = jnp.tile(jnp.concatenate([-half_tables[1], half_tables[1]], axis=1), (1, 4))
        kv_bands = kw // BAND
        shapes = (micro, per_pack, kv_bands)
        cost = pl.CostEstimate(
            flops=100000000000, bytes_accessed=0, transcendentals=0
        )
        qkv, attended, n1_rel, gains_rel = kernel_call(
            functools.partial(forward_kernel, *shapes),
            [
                jax.ShapeDtypeStruct((rows, wide), bf16),
                jax.ShapeDtypeStruct((rows, qw), bf16),
                jax.ShapeDtypeStruct((rows, width), bf16),
                jax.ShapeDtypeStruct((8, width), f32),
            ],
            cost,
            x_rel,
            cos_band,
            sin_band,
            allowed,
            *q_pieces,
            *y_pieces,
        )
        g2 = restore(gains_rel[1:2].astype(bf16), pick_attn)
        (mlp_last,) = join_call((mlp_near,), [[(0, 0)]], [3 * ff], attended)
        mlp_y3 = swap(mlp_last, y_mask)
        att_rel, middle, n2_rel = kernel_call(
            output_kernel,
            [shape_of(rows, qw, bf16), shape_of(rows, width, f32), shape_of(rows, width, bf16)],
            estimate(6 * rows * width * width),
            attended,
            pick_out,
            x_low,
            g2,
            pick_mlp,
            *left_pieces,
            *right_pieces,
            token=mlp_last,
        )

        n2_x = swap(n2_rel, x_mask)
        n2_c = swap(n2_rel, core_mask)
        (dy_near,) = kernel_call(
            functools.partial(order_kernel, 2),
            [shape_of(2 * rows, width, bf16)],
            estimate(0),
            dy_low,
            dy_x,
            pick_mlp,
            token=n2_rel,
        )
        dy_c = swap(dy_near, core_mask)
        near_parts = (own_mlp, mlp_z, mlp_far, mlp_last)
        far_parts = (mlp_y, mlp_y1, mlp_y2, mlp_y3)
        for mask in z_masks[2:]:
            near_parts = near_parts + (swap(join(near_parts), mask),)
            far_parts = far_parts + (swap(near_parts[-1], y_mask),)

        def assemble(parts, token):
            plan = [[(k, 0) for k in range(len(parts))], [(k, 2 * ff) for k in range(len(parts))]]
            return join_call(parts, plan, (2 * ff, ff), token)

        gu_near, down_near = assemble(near_parts, dy_near)
        (n2_f,) = join_call((n2_x,), [[(0, 0)]], [width], (mlp_y2,) + far_parts[-1:] + (gu_near,))
        n2_xc = swap(n2_f, core_mask)
        gu_far, down_far = assemble(far_parts, n2_f)
        weights = (gu_near, gu_far, down_near, down_far)
        n2_all = [(n2_rel, 0), (n2_x, 0), (n2_c, 0), (n2_xc, 0)]
        dy_all = [(dy_near, 0), (dy_near, 1), (dy_c, 0), (dy_c, 1)]
        weights = (gu_near, gu_far, down_near, down_far)
        *grown, far_own, far_send = mlp_call(
            1, n2_all[1::2], dy_all[1::2], weights, gu_far
        )
        far_c = swap(far_send, core_mask)
        (dn2_sum,) = sum_call([far_own, far_c], [bf16], far_own)
        dn2_x = swap(dn2_sum, x_mask)
        hidden, dgu, near_own, near_send = mlp_call(
            0, n2_all[::2], dy_all[::2], weights, *grown, dn2_sum
        )
        near_c = swap(near_send, core_mask)
        down_b = sent_call(dy_all, hidden, 0, ff, near_own)
        down_got = swap(down_b, y_mask)

        dmid, dmb = kernel_call(
            second_norm_kernel,
            [shape_of(rows, width, f32), shape_of(rows, width, bf16)],
            estimate(4 * rows * width * width),
            near_own,
            near_c,
            dn2_x,
            pick_mlp,
            dy_low,
            middle,
            g2,
            token=down_b,
        )
        (dqkv,) = kernel_call(
            functools.partial(backward_kernel, *shapes),
            [shape_of(rows, wide, bf16)],
            cost,
            dmb,
            qkv,
            cos_band,
            sin_band,
            allowed,
            pick_out,
            *left_pieces,
            *right_pieces,
            scratch=[pltpu.VMEM((rows, qw), bf16)],
        )
        qkv_b = sent_call(n1_rel, dqkv, 0, wide, dqkv)
        qkv_c = swap(qkv_b, core_mask)
        gate_b = sent_call(n2_all, dgu, 0, ff, qkv_b)
        gate_got = swap(gate_b, y_mask)
        far_mask, near_mask = z_masks[-1], z_masks[-2]
        step = [f32, bf16]

        def onward(pair, got, mask, token):
            pair = sum_call([pair[0], got], step, token)
            return pair, swap(pair[1], mask)

        qkv_k = kept_call(n1_rel, dqkv, 0, wide, qkv_c, gate_b)
        qkv_got = swap(qkv_k[1], x_mask)
        down_k = kept_call(dy_all, hidden, 0, ff, down_got, qkv_k[0])
        down_got = swap(down_k[1], far_mask)
        up_b = sent_call(n2_all, dgu, ff, ff, down_k[0])
        up_got = swap(up_b, y_mask)
        gate_k = kept_call(n2_all, dgu, 0, ff, gate_got, up_b)
        gate_got = swap(gate_k[1], far_mask)
        (input_grad,) = kernel_call(
            functools.partial(first_norm_kernel, 2 * BAND),
            [shape_of(rows, width, f32)],
            estimate(2 * rows * width * (wide + 2 * width)),
            dqkv,
            x_rel,
            gains_rel,
            pick_attn,
            dmid,
            *q_pieces,
            *y_pieces,
            token=gate_k[0],
        )
        down_k, down_got = onward(down_k, down_got, near_mask, input_grad)
        gate_k, gate_got = onward(gate_k, gate_got, near_mask, down_k[0])
        up_k = kept_call(n2_all, dgu, ff, ff, up_got, gate_k[0])
        up_got = swap(up_k[1], far_mask)
        og_b = sent_call(att_rel, dmb, 0, width, up_k[0])
        og_c = swap(og_b, core_mask)
        lay = down_call(hidden, *weights[2:], og_b)
        lay_f = swap(lay[3], core_mask)
        down_grad = finish([down_k[0], down_got], lay[0])
        qkv_k, qkv_got = onward(qkv_k, qkv_got, y_mask, down_grad)
        og = kept_call(att_rel, dmb, 0, width, og_c, qkv_k[0])
        og_got = swap(og[1], x_mask)
        gate_grad = finish([gate_k[0], gate_got], og[0])
        up_k, up_got = onward(up_k, up_got, near_mask, gate_grad)
        qkv_k, qkv_got = onward(qkv_k, qkv_got, far_mask, up_k[0])
        og, og_got = onward(og, og_got, y_mask, qkv_k[0])
        (lay_s,) = sum_call([lay[1], lay_f], [bf16], og[0])
        lay_x = swap(lay_s, x_mask)
        og, og_got = onward(og, og_got, far_mask, lay_s)
        lay_c = swap(after(lay[2], og[0]), core_mask)
        up_grad = finish([up_k[0], up_got], og[0])
        qkv_k, qkv_got = onward(qkv_k, qkv_got, near_mask, up_grad)
        og, og_got = onward(og, og_got, near_mask, qkv_k[0])
        qkv_grad = finish([qkv_k[0], qkv_got], og[0])
        output_grad = finish([og[0], og_got], qkv_grad)
        (layer_out,) = kernel_call(
            layer_kernel,
            [shape_of(rows, width, bf16)],
            estimate(2 * rows * width * width),
            lay[0],
            lay_c,
            lay_x,
            pick_mlp,
            middle,
            token=output_grad,
        )
        q_grad, kv_grad = qkv_grad[:, :qw], qkv_grad[:, qw:]
        down_grad = down_grad.T

        first = jnp.sum(own_attn[:, :qw].astype(f32) * q_grad, axis=1)
        own_kv = own_attn[:, qw + width : qw + width + 2 * kw].astype(f32)
        first = first + jnp.sum(own_kv * kv_grad, axis=1)
        first_gain_grad = first / first_gain.astype(f32)
        second = jnp.sum(
            gate_weight.astype(f32) * gate_grad + up_weight.astype(f32) * up_grad, axis=1
        )
        for mask in t_masks:
            second = second + swap(second, mask)
        second = lax.dynamic_slice(second, (t_i * shard,), (shard,))
        second_gain_grad = second / second_gain.astype(f32)

        return (
            layer_out.reshape(tokens.shape),
            input_grad.reshape(tokens.shape),
            first_gain_grad,
            q_grad.reshape(shard, GROUP, KV_HEADS, HEAD).swapaxes(1, 2).reshape(shard, qw),
            kv_grad[:, :kw],
            kv_grad[:, kw:],
            output_grad,
            second_gain_grad,
            gate_grad,
            up_grad,
            down_grad,
        )

    return per_device


def solution(mesh):
    rows = P(None, AXES, None)
    split = P(AXES, None)
    placed = (
        rows,
        rows,
        P(AXES),
        split,
        split,
        split,
        split,
        P(AXES),
        P("dp", "tensor"),
        P("dp", "tensor"),
        P("tensor", "dp"),
        rows,
    )
    return jax.shard_map(
        program(dict(mesh.shape)),
        mesh=mesh,
        in_specs=placed,
        out_specs=(
            rows,
            rows,
            P(AXES),
            split,
            split,
            split,
            split,
            P(AXES),
            P("dp", "tensor"),
            P("dp", "tensor"),
            P("tensor", "dp"),
        ),
        check_vma=False,
    )
```
